128 devices in a mesh: head: 16 (over y_lo, z, core), blk: 8 (over x, y_hi).
Axes of the slice: x: 4, y: 4 (y_hi: 2, y_lo: 2; y = y_hi * 2 + y_lo), z: 4, core: 2. Of those that a mesh axis runs over, the one named last changes fastest.
Arguments:
- query_head_matrix: bfloat16 [16384, 8192], P(('blk', 'head')), may hold values from -8 to 8
- key_matrix: bfloat16 [16384, 1024], P(('blk', 'head')), may hold values from -8 to 8
- value_matrix: bfloat16 [16384, 1024], P(('blk', 'head')), may hold values from -6 to 6
- output_gradient: bfloat16 [16384, 8192], P(('blk', 'head')), may hold values from -6 to 6
- span_lengths: int32 [62], replicated, may hold values from 1 to 512, 15872 in all
Outputs:
- attended: bfloat16 [16384, 8192], P(('blk', 'head'))
- query_grad: bfloat16 [16384, 8192], P(('blk', 'head'))
- key_gradient: bfloat16 [16384, 1024], P(('blk', 'head'))
- value_gradient: bfloat16 [16384, 1024], P(('blk', 'head'))
The draws below stay inside these ranges and needn't reach their ends.
Inputs may be any that keep to these rules, and one draw needn't show every extreme that they name: `span_lengths`: the 62 span lengths sum to 15872, and the longest span holds exactly 512 tokens.
All inputs are finite; a program needn't handle non-finite values.
Results may differ from the reference program's by a relative error of at most 0.02.
Values may be sent and summed in bfloat16 or wider, within the bound.
No kernel may reach another device: no remote copies, remote signals or barrier semaphores. Data moves between devices by JAX's collectives and lax.ppermute only.
A program may use at most 128 MiB of HBM per device.

```python
import math
import jax
import jax.numpy as jnp
import numpy as np
from jax import lax

QUERY_HEADS = 64
KEY_VALUE_HEADS = 8
HEAD_WIDTH = 128
MOST = 512
SEQUENCE_TOKENS = 16384
CTX = 15872
NCHUNK = 62
N_BLK = 8


def draw_query_head_matrix(key, part):
    unmodified_key = jax.random.fold_in(key, 11)
    value_entries = jnp.clip(jax.random.normal(unmodified_key, (SEQUENCE_TOKENS, QUERY_HEADS * HEAD_WIDTH), jnp.float32), -4.5, 4.5)
    return value_entries.astype(jnp.bfloat16)


def draw_key_matrix(key, part):
    unmodified_key = jax.random.fold_in(key, 12)
    value_entries = jnp.clip(jax.random.normal(unmodified_key, (SEQUENCE_TOKENS, KEY_VALUE_HEADS * HEAD_WIDTH), jnp.float32), -4.5, 4.5)
    return value_entries.astype(jnp.bfloat16)


def block_scale(key, shape, split, low, high):
    level = 1.0
    for dim, blocks in split:
        heights = jax.random.uniform(jax.random.fold_in(jax.random.fold_in(key, 6), dim), (blocks,), jnp.float32, low / len(split), high / len(split))
        level = level * jnp.repeat(jnp.exp(heights), shape[dim] // blocks).reshape((-1,) + (1,) * (len(shape) - 1 - dim))
    return level


def length_profile(number_of, total, bound, slope):
    weights = [(1 << 20) // math.isqrt(rank ** slope) + 1 for rank in range(2, number_of + 1)]
    rest, holding = total - bound - (number_of - 1), [1] * (number_of - 1)
    while rest > 0:
        candidates = [i for i in range(number_of - 1) if holding[i] < bound]
        mass, budget = sum([weights[i] for i in candidates]), rest
        for i in candidates:
            addition = min(bound - holding[i], max(1, budget * weights[i] // mass), rest)
            holding[i] = holding[i] + addition
            rest = rest - addition
    return np.array([bound] + holding)


def uneven_parts(stream_key, amount, total, most, lean):
    if amount == 2:
        one = jax.random.randint(stream_key, (), max(1, total - most), min(most, total - 1) + 1)
        return jnp.stack([one, total - one])
    tallies = jnp.asarray(length_profile(amount, total, most, lean), jnp.int32)
    twos = (amount - 1) // 2
    giver, taker = tallies[1:1 + 2 * twos:2], tallies[2:2 + 2 * twos:2]
    margin = jnp.minimum(giver - 1, most - taker)
    moved = jax.random.randint(jax.random.fold_in(stream_key, 1), (twos,), 0, 1 << 20) % (margin + 1)
    tallies = tallies.at[1:1 + 2 * twos:2].set(giver - moved).at[2:2 + 2 * twos:2].set(taker + moved)
    return tallies[jax.random.permutation(jax.random.fold_in(stream_key, 2), amount)]


def gaussian(stream_key, dims, spread, limit, cuts=(), kind=jnp.bfloat16):
    values = spread * jax.random.normal(stream_key, dims, jnp.float32)
    if cuts:
        values = values * block_scale(stream_key, dims, cuts, -0.22, 0.18)
    return jnp.clip(values, -limit, limit).astype(kind)


def setup_inputs(seed: int = 0) -> dict:
    key_list = jax.random.split(jax.random.key(seed), 6)
    return {
        "query_head_matrix": draw_query_head_matrix(jax.random.fold_in(key_list[5], 71), 0),
        "key_matrix": draw_key_matrix(jax.random.fold_in(key_list[5], 71), 0),
        "value_matrix": gaussian(key_list[2], (SEQUENCE_TOKENS, KEY_VALUE_HEADS * HEAD_WIDTH), 1.0, 6.0, ((0, 128),)),
        "output_gradient": gaussian(key_list[3], (SEQUENCE_TOKENS, QUERY_HEADS * HEAD_WIDTH), 1.0, 6.0, ((0, 128),)),
        "span_lengths": uneven_parts(key_list[4], NCHUNK, CTX, MOST, 1).astype(jnp.int32),
    }


masked_score = -1e+30

def rounded(value_entries):
    return lax.optimization_barrier(value_entries.astype(jnp.bfloat16)).astype(jnp.float32)

def segment_of(span_lengths, positions):
    starts = jnp.cumsum(span_lengths) - span_lengths
    found_index = lax.optimization_barrier(jnp.sum((starts[None, :] <= positions[:, None]).astype(jnp.int32), axis=1)) - 1
    return jnp.where(positions >= CTX, NCHUNK, found_index).astype(jnp.int32)

def reference(query_head_matrix, key_matrix, value_matrix, output_gradient, span_lengths):
    group_width = QUERY_HEADS // KEY_VALUE_HEADS
    tile_rows = min(512, SEQUENCE_TOKENS // N_BLK)
    tile_total = SEQUENCE_TOKENS // tile_rows
    score_scale = 1.0 / math.sqrt(HEAD_WIDTH)
    positions = jnp.arange(SEQUENCE_TOKENS, dtype=jnp.int32)
    window_pos = jnp.arange(SEQUENCE_TOKENS + MOST, dtype=jnp.int32) - MOST
    query_seg = segment_of(span_lengths, positions)
    window_seg = segment_of(span_lengths, window_pos)
    question_visible = positions[None, :] <= positions[CTX:][:, None]

    def head_group(operands):
        query_group, key_one, value_one, grad_group = operands
        zeros_rim = jnp.zeros((MOST, HEAD_WIDTH), jnp.float32)
        key_window = jnp.concatenate([zeros_rim, key_one.astype(jnp.float32)])
        value_window = jnp.concatenate([zeros_rim, value_one.astype(jnp.float32)])
        query_float = query_group.astype(jnp.float32)
        grad_float = grad_group.astype(jnp.float32)

        def tile_setup(tile_index):
            first_row = tile_index * tile_rows
            window_rows = tile_rows + MOST
            query_tile = lax.dynamic_slice_in_dim(query_float, first_row, tile_rows, 0)
            key_tile = lax.dynamic_slice_in_dim(key_window, first_row, window_rows, 0)
            value_tile = lax.dynamic_slice_in_dim(value_window, first_row, window_rows, 0)
            row_seg = lax.dynamic_slice_in_dim(query_seg, first_row, tile_rows, 0)
            row_pos = lax.dynamic_slice_in_dim(positions, first_row, tile_rows, 0)
            key_seg = lax.dynamic_slice_in_dim(window_seg, first_row, window_rows, 0)
            key_pos = lax.dynamic_slice_in_dim(window_pos, first_row, window_rows, 0)
            visible = (row_seg[:, None] == key_seg[None, :]) & (key_pos[None, :] <= row_pos[:, None]) & (row_seg[:, None] < NCHUNK)
            scores = jnp.einsum('qgd,kd->gqk', query_tile, key_tile) * score_scale
            scores = jnp.where(visible[None], scores, masked_score)
            return (first_row, query_tile, key_tile, value_tile, visible, scores)

        def forward_tile(tile_index):
            first_row, query_tile, key_tile, value_tile, visible, scores = tile_setup(tile_index)
            row_max = lax.optimization_barrier(jnp.max(scores, axis=2))
            weights = jnp.where(visible[None], jnp.exp(scores - row_max[..., None]), 0.0)
            row_total = lax.optimization_barrier(jnp.sum(weights, axis=2))
            summed = jnp.einsum('gqk,kd->qgd', rounded(weights), value_tile)
            return (row_max.T, row_total.T, summed)
        tile_max, tile_sum, tile_acc = lax.map(forward_tile, jnp.arange(tile_total))
        tile_max = tile_max.reshape(SEQUENCE_TOKENS, group_width)
        tile_sum = tile_sum.reshape(SEQUENCE_TOKENS, group_width)
        tile_acc = tile_acc.reshape(SEQUENCE_TOKENS, group_width, HEAD_WIDTH)

        def question_forward(query_one):
            scores = jnp.dot(query_one, key_one.T, preferred_element_type=jnp.float32) * score_scale
            scores = jnp.where(question_visible, scores, masked_score)
            row_max = lax.optimization_barrier(jnp.max(scores, axis=1))
            weights = jnp.where(question_visible, jnp.exp(scores - row_max[:, None]), 0.0)
            row_total = lax.optimization_barrier(jnp.sum(weights, axis=1))
            summed = jnp.dot(weights.astype(jnp.bfloat16), value_one, preferred_element_type=jnp.float32)
            return (row_max, row_total, summed)
        question_query = jnp.moveaxis(query_group[CTX:], 1, 0)
        question_grad = jnp.moveaxis(grad_group[CTX:], 1, 0)
        quest_max, quest_sum, quest_acc = lax.map(question_forward, question_query)
        row_max = jnp.concatenate([tile_max[:CTX], quest_max.T])
        row_total = jnp.concatenate([tile_sum[:CTX], quest_sum.T])
        row_acc = jnp.concatenate([tile_acc[:CTX], jnp.moveaxis(quest_acc, 0, 1)])
        attended = (row_acc / row_total[..., None]).astype(jnp.bfloat16)
        row_lse = row_max + jnp.log(row_total)
        row_dd = lax.optimization_barrier(jnp.sum(grad_float * attended.astype(jnp.float32), axis=2))

        def backward_tile(running, tile_index):
            key_grads, value_grads = running
            first_row, query_tile, key_tile, value_tile, visible, scores = tile_setup(tile_index)
            lse_tile = lax.dynamic_slice_in_dim(row_lse, first_row, tile_rows, 0).T
            dd_tile = lax.dynamic_slice_in_dim(row_dd, first_row, tile_rows, 0).T
            grad_tile = lax.dynamic_slice_in_dim(grad_float, first_row, tile_rows, 0)
            probabilities = jnp.where(visible[None], jnp.exp(scores - lse_tile[..., None]), 0.0)
            value_part = jnp.einsum('gqk,qgd->kd', rounded(probabilities), grad_tile)
            prob_grad = jnp.einsum('qgd,kd->gqk', grad_tile, value_tile)
            score_grad = rounded(probabilities * (prob_grad - dd_tile[..., None]))
            query_part = jnp.einsum('gqk,kd->qgd', score_grad, key_tile) * score_scale
            key_part = jnp.einsum('gqk,qgd->kd', score_grad, query_tile) * score_scale
            window_rows = tile_rows + MOST
            key_grads = lax.dynamic_update_slice_in_dim(key_grads, lax.dynamic_slice_in_dim(key_grads, first_row, window_rows, 0) + key_part, first_row, 0)
            value_grads = lax.dynamic_update_slice_in_dim(value_grads, lax.dynamic_slice_in_dim(value_grads, first_row, window_rows, 0) + value_part, first_row, 0)
            return ((key_grads, value_grads), query_part)
        empty_window = jnp.zeros((SEQUENCE_TOKENS + MOST, HEAD_WIDTH), jnp.float32)
        (key_grads, value_grads), query_tiles = lax.scan(backward_tile, (empty_window, empty_window), jnp.arange(tile_total))
        query_tiles = query_tiles.reshape(SEQUENCE_TOKENS, group_width, HEAD_WIDTH)

        def question_backward(parts):
            query_one, grad_one, lse_one, dd_one = parts
            scores = jnp.dot(query_one, key_one.T, preferred_element_type=jnp.float32) * score_scale
            probabilities = jnp.where(question_visible, jnp.exp(scores - lse_one[:, None]), 0.0)
            value_part = jnp.dot(probabilities.astype(jnp.bfloat16).T, grad_one, preferred_element_type=jnp.float32)
            prob_grad = jnp.dot(grad_one, value_one.T, preferred_element_type=jnp.float32)
            score_grad = (probabilities * (prob_grad - dd_one[:, None])).astype(jnp.bfloat16)
            query_part = jnp.dot(score_grad, key_one, preferred_element_type=jnp.float32) * score_scale
            key_part = jnp.dot(score_grad.T, query_one, preferred_element_type=jnp.float32) * score_scale
            return (query_part, key_part, value_part)
        quest_query_grad, quest_key_grad, quest_value_grad = lax.map(question_backward, (question_query, question_grad, row_lse[CTX:].T, row_dd[CTX:].T))
        query_grad = jnp.concatenate([query_tiles[:CTX], query_tiles[CTX:] + jnp.moveaxis(quest_query_grad, 0, 1)])
        key_gradient = key_grads[MOST:] + lax.optimization_barrier(jnp.sum(quest_key_grad, axis=0))
        value_gradient = value_grads[MOST:] + lax.optimization_barrier(jnp.sum(quest_value_grad, axis=0))
        return (attended, query_grad.astype(jnp.bfloat16), key_gradient.astype(jnp.bfloat16), value_gradient.astype(jnp.bfloat16))
    query_matrix = jnp.moveaxis(query_head_matrix.reshape(SEQUENCE_TOKENS, KEY_VALUE_HEADS, group_width, HEAD_WIDTH), 1, 0)
    output_adjoint = jnp.moveaxis(output_gradient.reshape(SEQUENCE_TOKENS, KEY_VALUE_HEADS, group_width, HEAD_WIDTH), 1, 0)
    key_head_rows = jnp.moveaxis(key_matrix.reshape(SEQUENCE_TOKENS, KEY_VALUE_HEADS, HEAD_WIDTH), 1, 0)
    value_head_rows = jnp.moveaxis(value_matrix.reshape(SEQUENCE_TOKENS, KEY_VALUE_HEADS, HEAD_WIDTH), 1, 0)
    attended, query_grad, key_gradient, value_gradient = lax.map(head_group, (query_matrix, key_head_rows, value_head_rows, output_adjoint))
    attended = jnp.moveaxis(attended, 0, 1).reshape(SEQUENCE_TOKENS, QUERY_HEADS * HEAD_WIDTH)
    query_grad = jnp.moveaxis(query_grad, 0, 1).reshape(SEQUENCE_TOKENS, QUERY_HEADS * HEAD_WIDTH)
    key_gradient = jnp.moveaxis(key_gradient, 0, 1).reshape(SEQUENCE_TOKENS, KEY_VALUE_HEADS * HEAD_WIDTH)
    value_gradient = jnp.moveaxis(value_gradient, 0, 1).reshape(SEQUENCE_TOKENS, KEY_VALUE_HEADS * HEAD_WIDTH)
    return (attended, query_grad, key_gradient, value_gradient)
```

```python
import functools
import math

import jax
import jax.numpy as jnp
from jax import lax
from jax.experimental import pallas as pl
from jax.experimental.pallas import tpu as pltpu
from jax.sharding import Mesh
from jax.sharding import PartitionSpec as P

QUERY_HEADS = 64
KEY_VALUE_HEADS = 8
HEAD_WIDTH = 128
GROUP = QUERY_HEADS // KEY_VALUE_HEADS
QLEN = 512
ROWS = 128
BACK = 4
SPANS = 62
AXES = ("x", "yh", "yl", "z", "c")
MESH_AXES = ("yl", "z", "c", "x", "yh")
PLANE = ("x", "yh", "yl")
DEVICES = 128
CONTEXT = DEVICES * ROWS - QLEN
RING = 8 * ROWS
SCALE = 1.0 / math.sqrt(HEAD_WIDTH)
SCALE2 = SCALE * math.log2(math.e)
HIDDEN = -1e30
FLOOR = -1e29
BF16 = jnp.bfloat16
F32 = jnp.float32


def dot_nt(a, b):
    return lax.dot_general(a, b, (((1,), (1,)), ((), ())), preferred_element_type=F32)


def dot_nn(a, b):
    return lax.dot_general(a, b, (((1,), (0,)), ((), ())), preferred_element_type=F32)


def stacked(pair):
    return jnp.concatenate([pair[:, :HEAD_WIDTH], pair[:, HEAD_WIDTH:]], axis=0)


def unstacked(transposed):
    rows = transposed.T
    return jnp.concatenate([rows[:ROWS], rows[ROWS:]], axis=1).astype(BF16)


def context_kernel(
    place_ref, span_ref, q_ref, g_ref, kv0, kv1, kv2, kv3, kv4,
    out_ref, dq_ref, d0, d1, d2, d3, d4,
    bias, k_win, v_win, k_t, v_t, dk_acc, dv_acc,
):
    window = (BACK + 1) * ROWS
    group, pair = pl.program_id(0), pl.program_id(1)
    place = place_ref[0]

    @pl.when((group == 0) & (pair == 0))
    def _():
        row = place * ROWS + lax.broadcasted_iota(jnp.int32, (1, ROWS), 1)

        def step(n, carry):
            begin, start = carry
            start = jnp.where(row >= begin, begin, start)
            return begin + span_ref[n], start

        _, start = lax.fori_loop(0, SPANS, step, (jnp.int32(0), jnp.zeros((1, ROWS), jnp.int32)))
        start = jnp.where(row >= CONTEXT, DEVICES * ROWS, start)
        key = (place - BACK) * ROWS + lax.broadcasted_iota(jnp.int32, (window, ROWS), 0)
        bias[...] = jnp.where((key >= start) & (key <= row), 0.0, HIDDEN)

    @pl.when(pair == 0)
    def _():
        for i, ref in enumerate((kv4, kv3, kv2, kv1, kv0)):
            k_win[i * ROWS : (i + 1) * ROWS] = ref[0, 0]
            v_win[i * ROWS : (i + 1) * ROWS] = ref[0, 1]
            k_t[:, i * ROWS : (i + 1) * ROWS] = ref[0, 0].T
            v_t[:, i * ROWS : (i + 1) * ROWS] = ref[0, 1].T
        dk_acc[...] = jnp.zeros_like(dk_acc)
        dv_acc[...] = jnp.zeros_like(dv_acc)

    q = stacked(q_ref[...])
    g = stacked(g_ref[...])
    hide = jnp.concatenate([bias[...], bias[...]], axis=1)
    s = dot_nt(k_win[...], q) * SCALE2 + hide
    top = jnp.maximum(jnp.max(s, axis=0, keepdims=True), FLOOR)
    w = jnp.exp2(s - top)
    total = jnp.sum(w, axis=0, keepdims=True)
    p = w * jnp.where(total > 0.0, 1.0 / total, 0.0)
    dp = dot_nt(v_win[...], g)
    dd = jnp.sum(p * dp, axis=0, keepdims=True)
    ds = (p * (dp - dd)).astype(BF16)
    pb = p.astype(BF16)
    out_ref[...] = unstacked(dot_nn(v_t[...], pb))
    dq_ref[...] = unstacked(dot_nn(k_t[...], ds) * SCALE)
    dv_acc[...] += dot_nn(pb, g)
    dk_acc[...] += dot_nn(ds, q)

    @pl.when(pair == GROUP // 2 - 1)
    def _():
        for i, ref in enumerate((d4, d3, d2, d1, d0)):
            ref[0, 0] = (dk_acc[i * ROWS : (i + 1) * ROWS] * SCALE).astype(BF16)
            ref[0, 1] = dv_acc[i * ROWS : (i + 1) * ROWS].astype(BF16)


def context_attention(place, span_lengths, q, g, blocks):
    window = (BACK + 1) * ROWS
    wide = pl.BlockSpec((ROWS, 2 * HEAD_WIDTH), lambda a, b, *_: (0, a * (GROUP // 2) + b))
    block = pl.BlockSpec((1, 2, ROWS, HEAD_WIDTH), lambda a, b, *_: (a, 0, 0, 0))
    whole = jax.ShapeDtypeStruct(q.shape, BF16)
    part = jax.ShapeDtypeStruct((KEY_VALUE_HEADS, 2, ROWS, HEAD_WIDTH), BF16)
    return pl.pallas_call(
        context_kernel,
        grid_spec=pltpu.PrefetchScalarGridSpec(
            num_scalar_prefetch=2,
            grid=(KEY_VALUE_HEADS, GROUP // 2),
            in_specs=[wide, wide] + [block] * 5,
            out_specs=[wide, wide] + [block] * 5,
            scratch_shapes=[
                pltpu.VMEM((window, ROWS), F32),
                pltpu.VMEM((window, HEAD_WIDTH), BF16),
                pltpu.VMEM((window, HEAD_WIDTH), BF16),
                pltpu.VMEM((HEAD_WIDTH, window), BF16),
                pltpu.VMEM((HEAD_WIDTH, window), BF16),
                pltpu.VMEM((window, HEAD_WIDTH), F32),
                pltpu.VMEM((window, HEAD_WIDTH), F32),
            ],
        ),
        out_shape=[whole, whole] + [part] * 5,
        name="context_rows",
    )(place, span_lengths, q, g, *blocks)


def question_scores(ring_ref, k, q, half):
    wide = q.shape[0]
    s = dot_nt(k, q) * SCALE2
    r = half * wide + lax.broadcasted_iota(jnp.int32, (1, wide), 1)
    row = CONTEXT + (r // 8) % 4 * ROWS + r // 32 * 8 + r % 8
    key = ring_ref[0] * RING + lax.broadcasted_iota(jnp.int32, s.shape, 0)
    return jnp.where(key <= row, s, HIDDEN)


def question_half(qg_ref, half, which):
    part = qg_ref[:, which]
    return part.reshape(part.shape[0] * part.shape[1], HEAD_WIDTH)


def statistics_kernel(ring_ref, qg_ref, kv_ref, stats_ref):
    head, half = pl.program_id(0), pl.program_id(1)
    k = kv_ref[:, 0].reshape(RING, HEAD_WIDTH)
    v = kv_ref[:, 1].reshape(RING, HEAD_WIDTH)
    q = question_half(qg_ref, half, 0)
    g = question_half(qg_ref, half, 1)
    s = question_scores(ring_ref, k, q, half)
    top = jnp.max(s, axis=0, keepdims=True)
    w = jnp.exp2(s - top)
    total = jnp.sum(w, axis=0, keepdims=True)
    dd = jnp.sum(w * dot_nt(v, g), axis=0, keepdims=True)
    stats_ref[pl.ds(head, 1), :] = top
    stats_ref[pl.ds(GROUP + head, 1), :] = total
    stats_ref[pl.ds(2 * GROUP + head, 1), :] = dd


def question_kernel(ring_ref, qg_ref, kv_ref, stats_ref, part_ref, dkv_ref, k_t, v_t, dk_acc, dv_acc):
    head, half = pl.program_id(0), pl.program_id(1)
    k = kv_ref[:, 0].reshape(RING, HEAD_WIDTH)
    v = kv_ref[:, 1].reshape(RING, HEAD_WIDTH)

    @pl.when((head == 0) & (half == 0))
    def _():
        k_t[...] = k.T
        v_t[...] = v.T
        dk_acc[...] = jnp.zeros_like(dk_acc)
        dv_acc[...] = jnp.zeros_like(dv_acc)

    q = question_half(qg_ref, half, 0)
    g = question_half(qg_ref, half, 1)
    s = question_scores(ring_ref, k, q, half)
    lse = stats_ref[pl.ds(head, 1), :]
    dd = stats_ref[pl.ds(GROUP + head, 1), :]
    p = jnp.exp2(s - lse)
    ds = (p * (dot_nt(v, g) - dd)).astype(BF16)
    pb = p.astype(BF16)
    shape = (part_ref.shape[0], part_ref.shape[2], HEAD_WIDTH)
    part_ref[:, 0] = dot_nn(v_t[...], pb).T.astype(BF16).reshape(shape)
    part_ref[:, 1] = (dot_nn(k_t[...], ds) * SCALE).T.astype(BF16).reshape(shape)
    dv_acc[...] += dot_nn(pb, g)
    dk_acc[...] += dot_nn(ds, q)

    @pl.when((head == GROUP - 1) & (half == 1))
    def _():
        dkv_ref[:, 0] = (dk_acc[...] * SCALE).astype(BF16).reshape(8, ROWS, HEAD_WIDTH)
        dkv_ref[:, 1] = dv_acc[...].astype(BF16).reshape(8, ROWS, HEAD_WIDTH)


def question_specs():
    rows = pl.BlockSpec((8, 2, 32, HEAD_WIDTH), lambda h, c, *_: (c, 0, 0, h))
    keys = pl.BlockSpec((8, 2, ROWS, HEAD_WIDTH), lambda h, c, *_: (0, 0, 0, 0))
    return rows, keys


def question_statistics(ring, qg, kv):
    rows, keys = question_specs()
    return pl.pallas_call(
        statistics_kernel,
        grid_spec=pltpu.PrefetchScalarGridSpec(
            num_scalar_prefetch=1,
            grid=(GROUP, 2),
            in_specs=[rows, keys],
            out_specs=pl.BlockSpec((3 * GROUP, QLEN // 2), lambda h, c, *_: (0, c)),
        ),
        out_shape=jax.ShapeDtypeStruct((3 * GROUP, QLEN), F32),
        name="question_statistics",
    )(ring, qg, kv)


def question_attention(ring, qg, kv, stats):
    rows, keys = question_specs()
    return pl.pallas_call(
        question_kernel,
        grid_spec=pltpu.PrefetchScalarGridSpec(
            num_scalar_prefetch=1,
            grid=(GROUP, 2),
            in_specs=[rows, keys, pl.BlockSpec((2 * GROUP, QLEN // 2), lambda h, c, *_: (0, c))],
            out_specs=[rows, keys],
            scratch_shapes=[
                pltpu.VMEM((HEAD_WIDTH, RING), BF16),
                pltpu.VMEM((HEAD_WIDTH, RING), BF16),
                pltpu.VMEM((RING, HEAD_WIDTH), F32),
                pltpu.VMEM((RING, HEAD_WIDTH), F32),
            ],
        ),
        out_shape=[
            jax.ShapeDtypeStruct(qg.shape, BF16),
            jax.ShapeDtypeStruct(kv.shape, BF16),
        ],
        name="question_rows",
    )(ring, qg, kv, stats)


def shifted(block, distance):
    index = [place % 16 * 8 + place // 16 for place in range(DEVICES)]
    route = [(index[i], index[(i + distance) % DEVICES]) for i in range(DEVICES)]
    return lax.ppermute(block, MESH_AXES, route)


def exchanged(blocks, axes):
    return lax.all_to_all(blocks, axes, split_axis=0, concat_axis=0, tiled=True)


def merged(stats, axis):
    parts = lax.all_gather(stats, axis)
    tops, totals, sums = jnp.split(parts, 3, axis=1)
    top = jnp.max(tops, axis=0)
    factor = jnp.exp2(tops - top)
    return jnp.concatenate([top, jnp.sum(totals * factor, axis=0), jnp.sum(sums * factor, axis=0)])


def shards(q, k, v, g, span_lengths):
    place = lax.axis_index(AXES)
    ring = place // 8
    ring_arg = ring.reshape(1).astype(jnp.int32)
    place_arg = place.reshape(1).astype(jnp.int32)
    last = place >= DEVICES - 4

    def dealt(a):
        return a.reshape(16, 8, KEY_VALUE_HEADS, GROUP * HEAD_WIDTH).transpose(0, 2, 1, 3)

    deal = jnp.stack([dealt(q), dealt(g)], axis=2).reshape(DEVICES, 2, 8, GROUP * HEAD_WIDTH)
    own = exchanged(deal, AXES)[DEVICES - 4 :]
    own = own.transpose(1, 0, 2, 3).reshape(1, 2, 32, GROUP * HEAD_WIDTH)
    qg = exchanged(jnp.broadcast_to(own, (16,) + own.shape[1:]), PLANE)

    def headed(a):
        return a.reshape(ROWS, KEY_VALUE_HEADS, HEAD_WIDTH).transpose(1, 0, 2)

    kv = jnp.stack([headed(k), headed(v)], axis=1)
    kv_ring = exchanged(kv, ("z", "c"))
    kv1, kv2 = shifted(kv, 1), shifted(kv, 2)
    kv3, kv4 = shifted(kv1, 2), shifted(kv2, 2)

    out, dq, d0, d1, d2, d3, d4 = context_attention(
        place_arg, span_lengths, q, g, (kv, kv1, kv2, kv3, kv4)
    )
    stats = merged(merged(question_statistics(ring_arg, qg, kv_ring), ("yh", "yl")), "x")
    top, total, sums = jnp.split(stats, 3)
    stats = jnp.concatenate([top + jnp.log2(total), sums / total])
    parts, dkv_ring = question_attention(ring_arg, qg, kv_ring, stats)

    def added(*terms):
        return sum(t.astype(F32) for t in terms)

    r3, r4 = shifted(d3, -2), shifted(d4, -2)
    r1 = shifted(added(d1, r3).astype(BF16), -1)
    r2 = shifted(added(d2, r4).astype(BF16), -2)
    dkv = added(d0, r1, r2, exchanged(dkv_ring, ("z", "c"))).astype(BF16)
    dk = dkv[:, 0].transpose(1, 0, 2).reshape(k.shape)
    dv = dkv[:, 1].transpose(1, 0, 2).reshape(v.shape)

    summed = jnp.sum(exchanged(parts, PLANE).astype(F32), axis=0).astype(BF16)
    summed = summed.reshape(2, 4, 8, GROUP * HEAD_WIDTH).transpose(1, 0, 2, 3)
    rest = jnp.zeros((DEVICES - 4,) + summed.shape[1:], BF16)
    back = exchanged(jnp.concatenate([rest, summed]), AXES)
    back = back.reshape(16, KEY_VALUE_HEADS, 2, 8, GROUP * HEAD_WIDTH).transpose(2, 0, 3, 1, 4)
    back = back.reshape(2, ROWS, QUERY_HEADS * HEAD_WIDTH)
    return jnp.where(last, back[0], out), jnp.where(last, back[1], dq), dk, dv


def solution(mesh):
    grid = Mesh(mesh.devices.reshape(2, 4, 2, 4, 2), MESH_AXES)
    rows = P(AXES, None)
    return jax.shard_map(
        shards,
        mesh=grid,
        in_specs=(rows, rows, rows, rows, P()),
        out_specs=(rows,) * 4,
        check_vma=False,
    )
```

```python
import math

import jax
import jax.numpy as jnp
from jax import lax
from jax.experimental import pallas as pl
from jax.experimental.pallas import tpu as pltpu
from jax.sharding import Mesh
from jax.sharding import PartitionSpec as P

QUERY_HEADS = 64
KEY_VALUE_HEADS = 8
HEAD_WIDTH = 128
GROUP = QUERY_HEADS // KEY_VALUE_HEADS
QLEN = 512
ROWS = 128
BACK = 4
SPANS = 62
AXES = ("x", "yh", "yl", "z", "c")
MESH_AXES = ("yl", "z", "c", "x", "yh")
PLANE = ("x", "yh", "yl")
DEVICES = 128
CONTEXT = DEVICES * ROWS - QLEN
RING = 8 * ROWS
SCALE = 1.0 / math.sqrt(HEAD_WIDTH)
SCALE2 = SCALE * math.log2(math.e)
HIDDEN = -1e30
FLOOR = -1e29
BF16 = jnp.bfloat16
F32 = jnp.float32


def dot_nt(a, b):
    return lax.dot_general(a, b, (((1,), (1,)), ((), ())), preferred_element_type=F32)


def dot_nn(a, b):
    return lax.dot_general(a, b, (((1,), (0,)), ((), ())), preferred_element_type=F32)


def stacked(pair):
    return jnp.concatenate([pair[:, :HEAD_WIDTH], pair[:, HEAD_WIDTH:]], axis=0)


def unstacked(transposed):
    rows = transposed.T
    return jnp.concatenate([rows[:ROWS], rows[ROWS:]], axis=1).astype(BF16)


def context_kernel(
    place_ref, span_ref, q_ref, g_ref, same0, same1, same2, swapped0, swapped1, swapped2, *rest,
):
    rest = rest[-14:]
    out_ref, dq_ref, d0, d1, d2, d3, d4, bias, k_win, v_win, k_t, v_t, dk_acc, dv_acc = rest
    window = (BACK + 1) * ROWS
    group, pair = pl.program_id(0), pl.program_id(1)
    place = place_ref[0]

    @pl.when((group == 0) & (pair == 0))
    def _():
        row = place * ROWS + lax.broadcasted_iota(jnp.int32, (1, ROWS), 1)

        def step(n, carry):
            begin, start = carry
            start = jnp.where(row >= begin, begin, start)
            return begin + span_ref[n], start

        _, start = lax.fori_loop(0, SPANS, step, (jnp.int32(0), jnp.zeros((1, ROWS), jnp.int32)))
        start = jnp.where(row >= CONTEXT, DEVICES * ROWS, start)
        key = (place - BACK) * ROWS + lax.broadcasted_iota(jnp.int32, (window, ROWS), 0)
        bias[...] = jnp.where((key >= start) & (key <= row), 0.0, HIDDEN)

    def fill(i, ref):
        k_win[i * ROWS : (i + 1) * ROWS] = ref[0, 0]
        v_win[i * ROWS : (i + 1) * ROWS] = ref[0, 1]
        k_t[:, i * ROWS : (i + 1) * ROWS] = ref[0, 0].T
        v_t[:, i * ROWS : (i + 1) * ROWS] = ref[0, 1].T

    @pl.when(pair == 0)
    def _():
        fill(0, same2)
        fill(2, same1)
        fill(4, same0)
        dk_acc[...] = jnp.zeros_like(dk_acc)
        dv_acc[...] = jnp.zeros_like(dv_acc)

    @pl.when((pair == 0) & (place % 2 == 0))
    def _():
        fill(1, swapped2)
        fill(3, swapped1)

    @pl.when((pair == 0) & (place % 2 == 1))
    def _():
        fill(1, swapped1)
        fill(3, swapped0)

    q = stacked(q_ref[...])
    g = stacked(g_ref[...])
    hide = jnp.concatenate([bias[...], bias[...]], axis=1)
    s = dot_nt(k_win[...], q) * SCALE2 + hide
    top = jnp.maximum(jnp.max(s, axis=0, keepdims=True), FLOOR)
    w = jnp.exp2(s - top)
    total = jnp.sum(w, axis=0, keepdims=True)
    p = w * jnp.where(total > 0.0, 1.0 / total, 0.0)
    dp = dot_nt(v_win[...], g)
    dd = jnp.sum(p * dp, axis=0, keepdims=True)
    ds = (p * (dp - dd)).astype(BF16)
    pb = p.astype(BF16)
    out_ref[...] = unstacked(dot_nn(v_t[...], pb))
    dq_ref[...] = unstacked(dot_nn(k_t[...], ds) * SCALE)
    dv_acc[...] += dot_nn(pb, g)
    dk_acc[...] += dot_nn(ds, q)

    @pl.when(pair == GROUP // 2 - 1)
    def _():
        for i, ref in enumerate((d4, d3, d2, d1, d0)):
            ref[0, 0] = (dk_acc[i * ROWS : (i + 1) * ROWS] * SCALE).astype(BF16)
            ref[0, 1] = dv_acc[i * ROWS : (i + 1) * ROWS].astype(BF16)


def context_attention(first, count, place, span_lengths, q, g, blocks, before=()):
    window = (BACK + 1) * ROWS
    wide = pl.BlockSpec((ROWS, 2 * HEAD_WIDTH), lambda a, b, *_: (0, (a + first) * (GROUP // 2) + b))
    block = pl.BlockSpec((1, 2, ROWS, HEAD_WIDTH), lambda a, b, *_: (a + first, 0, 0, 0))
    whole = jax.ShapeDtypeStruct(q.shape, BF16)
    part = jax.ShapeDtypeStruct((KEY_VALUE_HEADS, 2, ROWS, HEAD_WIDTH), BF16)
    return pl.pallas_call(
        context_kernel,
        grid_spec=pltpu.PrefetchScalarGridSpec(
            num_scalar_prefetch=2,
            grid=(count, GROUP // 2),
            in_specs=[wide, wide] + [block] * 6 + [pl.BlockSpec(memory_space=pl.ANY)] * len(before),
            out_specs=[wide, wide] + [block] * 5,
            scratch_shapes=[
                pltpu.VMEM((window, ROWS), F32),
                pltpu.VMEM((window, HEAD_WIDTH), BF16),
                pltpu.VMEM((window, HEAD_WIDTH), BF16),
                pltpu.VMEM((HEAD_WIDTH, window), BF16),
                pltpu.VMEM((HEAD_WIDTH, window), BF16),
                pltpu.VMEM((window, HEAD_WIDTH), F32),
                pltpu.VMEM((window, HEAD_WIDTH), F32),
            ],
        ),
        out_shape=[whole, whole] + [part] * 5,
        input_output_aliases={10 + i: i for i in range(len(before))},
        name="context_rows",
    )(place, span_lengths, q, g, *blocks, *before)


def question_scores(place_ref, ring, k, q):
    s = dot_nt(k, q) * SCALE2
    row = CONTEXT + place_ref[0] // 32 * ROWS + lax.broadcasted_iota(jnp.int32, (1, 2 * ROWS), 1) % ROWS
    key = ring_of(place_ref[0], ring) * RING + lax.broadcasted_iota(jnp.int32, s.shape, 0)
    return jnp.where(key <= row, s, HIDDEN)


def ring_of(place, ring):
    return (place // 32 + 4 - ring) % 4 * 4 + place // 8 % 4


def question_pair(qg_ref, which):
    return stacked(qg_ref[:, which].reshape(ROWS, 2 * HEAD_WIDTH))


def ring_keys(kv_ref):
    return kv_ref[0, :, 0].reshape(RING, HEAD_WIDTH), kv_ref[0, :, 1].reshape(RING, HEAD_WIDTH)


def statistics_kernel(place_ref, qg_ref, kv_ref, stats_ref):
    pair, ring = pl.program_id(0), pl.program_id(1)
    k, v = ring_keys(kv_ref)
    q = question_pair(qg_ref, 0)
    g = question_pair(qg_ref, 1)
    s = question_scores(place_ref, ring, k, q)
    slots = [pl.ds(pl.multiple_of(part * GROUP, GROUP) + pair, 1) for part in range(3)]

    @pl.when(ring == 0)
    def _():
        stats_ref[slots[0], :] = jnp.full((1, 2 * ROWS), FLOOR, F32)
        stats_ref[slots[1], :] = jnp.zeros((1, 2 * ROWS), F32)
        stats_ref[slots[2], :] = jnp.zeros((1, 2 * ROWS), F32)

    before = stats_ref[slots[0], :]
    top = jnp.maximum(before, jnp.max(s, axis=0, keepdims=True))
    factor = jnp.exp2(before - top)
    w = jnp.exp2(s - top)
    stats_ref[slots[0], :] = top
    stats_ref[slots[1], :] = stats_ref[slots[1], :] * factor + jnp.sum(w, axis=0, keepdims=True)
    dd = jnp.sum(w * dot_nt(v, g), axis=0, keepdims=True)
    stats_ref[slots[2], :] = stats_ref[slots[2], :] * factor + dd


def question_kernel(
    place_ref, qg_ref, kv_ref, stats_ref, part_ref, dkv_ref, k_t, v_t, dk_acc, dv_acc, out_acc, dq_acc
):
    ring, pair = pl.program_id(0), pl.program_id(1)
    k, v = ring_keys(kv_ref)

    @pl.when(pair == 0)
    def _():
        k_t[...] = k.T
        v_t[...] = v.T
        dk_acc[...] = jnp.zeros_like(dk_acc)
        dv_acc[...] = jnp.zeros_like(dv_acc)

    @pl.when(ring == 0)
    def _():
        out_acc[pair] = jnp.zeros((HEAD_WIDTH, 2 * ROWS), F32)
        dq_acc[pair] = jnp.zeros((HEAD_WIDTH, 2 * ROWS), F32)

    q = question_pair(qg_ref, 0)
    g = question_pair(qg_ref, 1)
    s = question_scores(place_ref, ring, k, q)
    lse = stats_ref[pl.ds(pair, 1), :]
    dd = stats_ref[pl.ds(GROUP + pair, 1), :]
    p = jnp.exp2(s - lse)
    ds = (p * (dot_nt(v, g) - dd)).astype(BF16)
    pb = p.astype(BF16)
    out_acc[pair] += dot_nn(v_t[...], pb)
    dq_acc[pair] += dot_nn(k_t[...], ds)
    dv_acc[...] += dot_nn(pb, g)
    dk_acc[...] += dot_nn(ds, q)

    @pl.when(ring == 3)
    def _():
        shape = (16, 8, 2 * HEAD_WIDTH)
        part_ref[:, 0] = unstacked(out_acc[pair]).reshape(shape)
        part_ref[:, 1] = unstacked(dq_acc[pair] * SCALE).reshape(shape)

    @pl.when(pair == GROUP // 2 - 1)
    def _():
        dkv_ref[0, :, 0] = (dk_acc[...] * SCALE).astype(BF16).reshape(8, ROWS, HEAD_WIDTH)
        dkv_ref[0, :, 1] = dv_acc[...].astype(BF16).reshape(8, ROWS, HEAD_WIDTH)


def question_statistics(place, qg, kv):
    return pl.pallas_call(
        statistics_kernel,
        grid_spec=pltpu.PrefetchScalarGridSpec(
            num_scalar_prefetch=1,
            grid=(GROUP // 2, 4),
            in_specs=[
                pl.BlockSpec((16, 2, 8, 2 * HEAD_WIDTH), lambda h, r, *_: (0, 0, 0, h)),
                pl.BlockSpec((1, 8, 2, ROWS, HEAD_WIDTH), lambda h, r, *_: (r, 0, 0, 0, 0)),
            ],
            out_specs=pl.BlockSpec((3 * GROUP, 2 * ROWS), lambda h, r, *_: (0, 0)),
        ),
        out_shape=jax.ShapeDtypeStruct((3 * GROUP, 2 * ROWS), F32),
        name="question_statistics",
    )(place, qg, kv)


def question_attention(place, qg, kv, stats):
    rows = pl.BlockSpec((16, 2, 8, 2 * HEAD_WIDTH), lambda r, h, *_: (0, 0, 0, h))
    keys = pl.BlockSpec((1, 8, 2, ROWS, HEAD_WIDTH), lambda r, h, *_: (r, 0, 0, 0, 0))
    last_rows = pl.BlockSpec(
        (16, 2, 8, 2 * HEAD_WIDTH), lambda r, h, *_: (0, 0, 0, jnp.where(r == 3, h, 0))
    )
    return pl.pallas_call(
        question_kernel,
        grid_spec=pltpu.PrefetchScalarGridSpec(
            num_scalar_prefetch=1,
            grid=(4, GROUP // 2),
            in_specs=[rows, keys, pl.BlockSpec((2 * GROUP, 2 * ROWS), lambda r, h, *_: (0, 0))],
            out_specs=[last_rows, keys],
            scratch_shapes=[
                pltpu.VMEM((HEAD_WIDTH, RING), BF16),
                pltpu.VMEM((HEAD_WIDTH, RING), BF16),
                pltpu.VMEM((RING, HEAD_WIDTH), F32),
                pltpu.VMEM((RING, HEAD_WIDTH), F32),
                pltpu.VMEM((GROUP // 2, HEAD_WIDTH, 2 * ROWS), F32),
                pltpu.VMEM((GROUP // 2, HEAD_WIDTH, 2 * ROWS), F32),
            ],
        ),
        out_shape=[
            jax.ShapeDtypeStruct(qg.shape, BF16),
            jax.ShapeDtypeStruct(kv.shape, BF16),
        ],
        name="question_rows",
    )(place, qg, kv, stats)


def permuted(block, target):
    index = [place % 16 * 8 + place // 16 for place in range(DEVICES)]
    route = [(index[i], index[target(i)]) for i in range(DEVICES)]
    return lax.ppermute(block, MESH_AXES, route)


def shifted(block, distance):
    return permuted(block, lambda i: (i + distance) % DEVICES)


def swapped(block):
    return permuted(block, lambda i: i ^ 1)


def exchanged(blocks, axes):
    return lax.all_to_all(blocks, axes, split_axis=0, concat_axis=0, tiled=True)


def merged(stats):
    parts = exchanged(jnp.broadcast_to(stats, (4,) + stats.shape), ("yh", "yl"))
    tops, totals, sums = jnp.split(parts, 3, axis=1)
    top = jnp.max(tops, axis=0)
    factor = jnp.exp2(tops - top)
    total = jnp.sum(totals * factor, axis=0)
    return jnp.concatenate([top + jnp.log2(total), jnp.sum(sums * factor, axis=0) / total])


def added(*terms):
    return sum(t.astype(F32) for t in terms)


def shards(q, k, v, g, span_lengths):
    place = lax.axis_index(AXES)
    place_arg = place.reshape(1).astype(jnp.int32)
    last = place >= DEVICES - 4
    even = place % 2 == 0
    wide = GROUP * HEAD_WIDTH

    def dealt(a):
        return a.reshape(16, 8, KEY_VALUE_HEADS, wide).transpose(0, 2, 1, 3)

    deal = jnp.stack([dealt(q), dealt(g)], axis=2).reshape(DEVICES, 2, 8, wide)
    deal = exchanged(deal, AXES)

    def headed(a):
        return a.reshape(ROWS, KEY_VALUE_HEADS, HEAD_WIDTH).transpose(1, 0, 2)

    kv = jnp.stack([headed(k), headed(v)], axis=1)
    same1 = shifted(kv, 2)
    same2 = shifted(same1, 2)
    blocks = (kv, same1, same2, swapped(kv), swapped(same1), swapped(same2))
    kv_ring = exchanged(kv, ("z", "c"))
    kv_ring = jnp.stack([kv_ring] + [shifted(kv_ring, 32 * i) for i in (1, 2, 3)])

    context = context_attention(0, 5, place_arg, span_lengths, q, g, blocks)
    deal, context = lax.optimization_barrier((deal, context))
    own = jnp.broadcast_to(deal[DEVICES - 4 :, None], (4, 4, 2, 8, wide))
    qg = exchanged(own.reshape(16, 2, 8, wide), PLANE)
    context = context_attention(5, 3, place_arg, span_lengths, q, g, blocks, context)
    qg, kv_ring, context = lax.optimization_barrier((qg, kv_ring, context))
    out, dq, d0, d1, d2, d3, d4 = context

    stats = merged(question_statistics(place_arg, qg, kv_ring))
    parts, dkv_ring = question_attention(place_arg, qg, kv_ring, stats)

    from1, from3 = swapped(d1), swapped(d3)
    none = jnp.zeros_like(d1)
    far = added(d4, jnp.where(even, none, from3)).astype(BF16)
    near = added(d2, jnp.where(even, from3, from1), shifted(far, -2)).astype(BF16)
    near = shifted(near, -2)
    dkv_ring = added(dkv_ring[0], *[shifted(dkv_ring[i], -32 * i) for i in (1, 2, 3)])
    dkv_ring = exchanged(dkv_ring.astype(BF16), ("z", "c"))
    dkv = added(d0, jnp.where(even, from1, none), near, dkv_ring).astype(BF16)
    dk = dkv[:, 0].transpose(1, 0, 2).reshape(k.shape)
    dv = dkv[:, 1].transpose(1, 0, 2).reshape(v.shape)

    parts = exchanged(parts, PLANE).reshape(4, 4, 2, 8, wide)
    summed = jnp.sum(parts.astype(F32), axis=1).astype(BF16)
    rest = jnp.zeros((DEVICES - 4,) + summed.shape[1:], BF16)
    back = exchanged(jnp.concatenate([rest, summed]), AXES)
    back = back.reshape(16, KEY_VALUE_HEADS, 2, 8, wide).transpose(2, 0, 3, 1, 4)
    back = back.reshape(2, ROWS, QUERY_HEADS * HEAD_WIDTH)
    return jnp.where(last, back[0], out), jnp.where(last, back[1], dq), dk, dv


def solution(mesh):
    grid = Mesh(mesh.devices.reshape(2, 4, 2, 4, 2), MESH_AXES)
    rows = P(AXES, None)
    return jax.shard_map(
        shards,
        mesh=grid,
        in_specs=(rows, rows, rows, rows, P()),
        out_specs=(rows,) * 4,
        check_vma=False,
    )
```

```python
import math

import jax
import jax.numpy as jnp
from jax import lax
from jax.experimental import pallas as pl
from jax.experimental.pallas import tpu as pltpu
from jax.sharding import Mesh
from jax.sharding import PartitionSpec as P

QUERY_HEADS = 64
KEY_VALUE_HEADS = 8
HEAD_WIDTH = 128
GROUP = QUERY_HEADS // KEY_VALUE_HEADS
QLEN = 512
ROWS = 128
BACK = 4
SPANS = 62
AXES = ("x", "yh", "yl", "z", "c")
MESH_AXES = ("yl", "z", "c", "x", "yh")
PLANE = ("x", "yh", "yl")
DEVICES = 128
CONTEXT = DEVICES * ROWS - QLEN
RING = 8 * ROWS
SCALE = 1.0 / math.sqrt(HEAD_WIDTH)
SCALE2 = SCALE * math.log2(math.e)
HIDDEN = -1e30
FLOOR = -1e29
BF16 = jnp.bfloat16
F32 = jnp.float32


def dot_nt(a, b):
    return lax.dot_general(a, b, (((1,), (1,)), ((), ())), preferred_element_type=F32)


def dot_nn(a, b):
    return lax.dot_general(a, b, (((1,), (0,)), ((), ())), preferred_element_type=F32)


def stacked(pair):
    return jnp.concatenate([pair[:, :HEAD_WIDTH], pair[:, HEAD_WIDTH:]], axis=0)


def unstacked(transposed):
    rows = transposed.T
    return jnp.concatenate([rows[:ROWS], rows[ROWS:]], axis=1).astype(BF16)


def context_kernel(
    place_ref, span_ref, q_ref, g_ref, same0, same1, same2, swapped0, swapped1, swapped2, *rest,
):
    rest = rest[-14:]
    out_ref, dq_ref, d0, d1, d2, d3, d4, bias, k_win, v_win, k_t, v_t, dk_acc, dv_acc = rest
    window = (BACK + 1) * ROWS
    group, pair = pl.program_id(0), pl.program_id(1)
    place = place_ref[0]

    @pl.when((group == 0) & (pair == 0))
    def _():
        row = place * ROWS + lax.broadcasted_iota(jnp.int32, (1, ROWS), 1)

        def step(n, carry):
            begin, start = carry
            start = jnp.where(row >= begin, begin, start)
            return begin + span_ref[n], start

        _, start = lax.fori_loop(0, SPANS, step, (jnp.int32(0), jnp.zeros((1, ROWS), jnp.int32)))
        start = jnp.where(row >= CONTEXT, DEVICES * ROWS, start)
        key = (place - BACK) * ROWS + lax.broadcasted_iota(jnp.int32, (window, ROWS), 0)
        bias[...] = jnp.where((key >= start) & (key <= row), 0.0, HIDDEN)

    def fill(i, ref):
        k_win[i * ROWS : (i + 1) * ROWS] = ref[0, 0]
        v_win[i * ROWS : (i + 1) * ROWS] = ref[0, 1]
        k_t[:, i * ROWS : (i + 1) * ROWS] = ref[0, 0].T
        v_t[:, i * ROWS : (i + 1) * ROWS] = ref[0, 1].T

    @pl.when(pair == 0)
    def _():
        fill(0, same2)
        fill(2, same1)
        fill(4, same0)
        dk_acc[...] = jnp.zeros_like(dk_acc)
        dv_acc[...] = jnp.zeros_like(dv_acc)

    @pl.when((pair == 0) & (place % 2 == 0))
    def _():
        fill(1, swapped2)
        fill(3, swapped1)

    @pl.when((pair == 0) & (place % 2 == 1))
    def _():
        fill(1, swapped1)
        fill(3, swapped0)

    q = stacked(q_ref[...])
    g = stacked(g_ref[...])
    hide = jnp.concatenate([bias[...], bias[...]], axis=1)
    s = dot_nt(k_win[...], q) * SCALE2 + hide
    top = jnp.maximum(jnp.max(s, axis=0, keepdims=True), FLOOR)
    w = jnp.exp2(s - top)
    total = jnp.sum(w, axis=0, keepdims=True)
    p = w * jnp.where(total > 0.0, 1.0 / total, 0.0)
    dp = dot_nt(v_win[...], g)
    dd = jnp.sum(p * dp, axis=0, keepdims=True)
    ds = (p * (dp - dd)).astype(BF16)
    pb = p.astype(BF16)
    out_ref[...] = unstacked(dot_nn(v_t[...], pb))
    dq_ref[...] = unstacked(dot_nn(k_t[...], ds) * SCALE)
    dv_acc[...] += dot_nn(pb, g)
    dk_acc[...] += dot_nn(ds, q)

    @pl.when(pair == GROUP // 2 - 1)
    def _():
        for i, ref in enumerate((d4, d3, d2, d1, d0)):
            ref[0, 0] = (dk_acc[i * ROWS : (i + 1) * ROWS] * SCALE).astype(BF16)
            ref[0, 1] = dv_acc[i * ROWS : (i + 1) * ROWS].astype(BF16)


def context_attention(first, count, place, span_lengths, q, g, blocks, before=()):
    window = (BACK + 1) * ROWS
    wide = pl.BlockSpec((ROWS, 2 * HEAD_WIDTH), lambda a, b, *_: (0, (a + first) * (GROUP // 2) + b))
    block = pl.BlockSpec((1, 2, ROWS, HEAD_WIDTH), lambda a, b, *_: (a + first, 0, 0, 0))
    whole = jax.ShapeDtypeStruct(q.shape, BF16)
    part = jax.ShapeDtypeStruct((KEY_VALUE_HEADS, 2, ROWS, HEAD_WIDTH), BF16)
    return pl.pallas_call(
        context_kernel,
        grid_spec=pltpu.PrefetchScalarGridSpec(
            num_scalar_prefetch=2,
            grid=(count, GROUP // 2),
            in_specs=[wide, wide] + [block] * 6 + [pl.BlockSpec(memory_space=pl.ANY)] * len(before),
            out_specs=[wide, wide] + [block] * 5,
            scratch_shapes=[
                pltpu.VMEM((window, ROWS), F32),
                pltpu.VMEM((window, HEAD_WIDTH), BF16),
                pltpu.VMEM((window, HEAD_WIDTH), BF16),
                pltpu.VMEM((HEAD_WIDTH, window), BF16),
                pltpu.VMEM((HEAD_WIDTH, window), BF16),
                pltpu.VMEM((window, HEAD_WIDTH), F32),
                pltpu.VMEM((window, HEAD_WIDTH), F32),
            ],
        ),
        out_shape=[whole, whole] + [part] * 5,
        input_output_aliases={10 + i: i for i in range(len(before))},
        name="context_rows",
    )(place, span_lengths, q, g, *blocks, *before)


def question_scores(place_ref, ring, k, q):
    s = dot_nt(k, q) * SCALE2
    lane = lax.broadcasted_iota(jnp.int32, (1, 2 * ROWS), 1) % ROWS
    x, y = lane // 32, lane // 8 % 4
    piece = jnp.where(x % 2 == 0, x * 2 + y, 8 + y // 2 * 4 + y % 2 + (3 - x))
    row = CONTEXT + place_ref[0] // 32 * ROWS + piece * 8 + lane % 8
    key = ring_of(place_ref[0], ring) * RING + lax.broadcasted_iota(jnp.int32, s.shape, 0)
    return jnp.where(key <= row, s, HIDDEN)


def ring_of(place, ring):
    return (place // 32 + 4 - ring) % 4 * 4 + place // 8 % 4


def question_pair(qg_ref, which):
    return stacked(qg_ref[:, which].reshape(ROWS, 2 * HEAD_WIDTH))


def ring_keys(kv_ref):
    return kv_ref[0, :, 0].reshape(RING, HEAD_WIDTH), kv_ref[0, :, 1].reshape(RING, HEAD_WIDTH)


def statistics_kernel(place_ref, qg_ref, kv_ref, stats_ref):
    pair, ring = pl.program_id(0), pl.program_id(1)
    k, v = ring_keys(kv_ref)
    q = question_pair(qg_ref, 0)
    g = question_pair(qg_ref, 1)
    s = question_scores(place_ref, ring, k, q)
    slots = [pl.ds(pl.multiple_of(part * GROUP, GROUP) + pair, 1) for part in range(3)]

    @pl.when(ring == 0)
    def _():
        stats_ref[slots[0], :] = jnp.full((1, 2 * ROWS), FLOOR, F32)
        stats_ref[slots[1], :] = jnp.zeros((1, 2 * ROWS), F32)
        stats_ref[slots[2], :] = jnp.zeros((1, 2 * ROWS), F32)

    before = stats_ref[slots[0], :]
    top = jnp.maximum(before, jnp.max(s, axis=0, keepdims=True))
    factor = jnp.exp2(before - top)
    w = jnp.exp2(s - top)
    stats_ref[slots[0], :] = top
    stats_ref[slots[1], :] = stats_ref[slots[1], :] * factor + jnp.sum(w, axis=0, keepdims=True)
    dd = jnp.sum(w * dot_nt(v, g), axis=0, keepdims=True)
    stats_ref[slots[2], :] = stats_ref[slots[2], :] * factor + dd


def question_kernel(
    place_ref, qg_ref, kv_ref, stats_ref, part_ref, dkv_ref, k_t, v_t, dk_acc, dv_acc, out_acc, dq_acc
):
    ring, pair = pl.program_id(0), pl.program_id(1)
    k, v = ring_keys(kv_ref)

    @pl.when(pair == 0)
    def _():
        k_t[...] = k.T
        v_t[...] = v.T
        dk_acc[...] = jnp.zeros_like(dk_acc)
        dv_acc[...] = jnp.zeros_like(dv_acc)

    @pl.when(ring == 0)
    def _():
        out_acc[pair] = jnp.zeros((HEAD_WIDTH, 2 * ROWS), F32)
        dq_acc[pair] = jnp.zeros((HEAD_WIDTH, 2 * ROWS), F32)

    q = question_pair(qg_ref, 0)
    g = question_pair(qg_ref, 1)
    s = question_scores(place_ref, ring, k, q)
    lse = stats_ref[pl.ds(pair, 1), :]
    dd = stats_ref[pl.ds(GROUP + pair, 1), :]
    p = jnp.exp2(s - lse)
    ds = (p * (dot_nt(v, g) - dd)).astype(BF16)
    pb = p.astype(BF16)
    out_acc[pair] += dot_nn(v_t[...], pb)
    dq_acc[pair] += dot_nn(k_t[...], ds)
    dv_acc[...] += dot_nn(pb, g)
    dk_acc[...] += dot_nn(ds, q)

    @pl.when(ring == 3)
    def _():
        shape = (16, 8, 2 * HEAD_WIDTH)
        part_ref[:, 0] = unstacked(out_acc[pair]).reshape(shape)
        part_ref[:, 1] = unstacked(dq_acc[pair] * SCALE).reshape(shape)

    @pl.when(pair == GROUP // 2 - 1)
    def _():
        dkv_ref[0, :, 0] = (dk_acc[...] * SCALE).astype(BF16).reshape(8, ROWS, HEAD_WIDTH)
        dkv_ref[0, :, 1] = dv_acc[...].astype(BF16).reshape(8, ROWS, HEAD_WIDTH)


def question_statistics(place, qg, kv):
    return pl.pallas_call(
        statistics_kernel,
        grid_spec=pltpu.PrefetchScalarGridSpec(
            num_scalar_prefetch=1,
            grid=(GROUP // 2, 4),
            in_specs=[
                pl.BlockSpec((16, 2, 8, 2 * HEAD_WIDTH), lambda h, r, *_: (0, 0, 0, h)),
                pl.BlockSpec((1, 8, 2, ROWS, HEAD_WIDTH), lambda h, r, *_: (r, 0, 0, 0, 0)),
            ],
            out_specs=pl.BlockSpec((3 * GROUP, 2 * ROWS), lambda h, r, *_: (0, 0)),
        ),
        out_shape=jax.ShapeDtypeStruct((3 * GROUP, 2 * ROWS), F32),
        name="question_statistics",
    )(place, qg, kv)


def question_attention(place, qg, kv, stats):
    rows = pl.BlockSpec((16, 2, 8, 2 * HEAD_WIDTH), lambda r, h, *_: (0, 0, 0, h))
    keys = pl.BlockSpec((1, 8, 2, ROWS, HEAD_WIDTH), lambda r, h, *_: (r, 0, 0, 0, 0))
    last_rows = pl.BlockSpec(
        (16, 2, 8, 2 * HEAD_WIDTH), lambda r, h, *_: (0, 0, 0, jnp.where(r == 3, h, 0))
    )
    return pl.pallas_call(
        question_kernel,
        grid_spec=pltpu.PrefetchScalarGridSpec(
            num_scalar_prefetch=1,
            grid=(4, GROUP // 2),
            in_specs=[rows, keys, pl.BlockSpec((2 * GROUP, 2 * ROWS), lambda r, h, *_: (0, 0))],
            out_specs=[last_rows, keys],
            scratch_shapes=[
                pltpu.VMEM((HEAD_WIDTH, RING), BF16),
                pltpu.VMEM((HEAD_WIDTH, RING), BF16),
                pltpu.VMEM((RING, HEAD_WIDTH), F32),
                pltpu.VMEM((RING, HEAD_WIDTH), F32),
                pltpu.VMEM((GROUP // 2, HEAD_WIDTH, 2 * ROWS), F32),
                pltpu.VMEM((GROUP // 2, HEAD_WIDTH, 2 * ROWS), F32),
            ],
        ),
        out_shape=[
            jax.ShapeDtypeStruct(qg.shape, BF16),
            jax.ShapeDtypeStruct(kv.shape, BF16),
        ],
        name="question_rows",
    )(place, qg, kv, stats)


def permuted(block, pairs):
    index = [place % 16 * 8 + place // 16 for place in range(DEVICES)]
    return lax.ppermute(block, MESH_AXES, [(index[i], index[j]) for i, j in pairs])


def shifted(block, distance):
    pairs = [(i, i + distance) for i in range(CONTEXT // ROWS)]
    return permuted(block, [(i, j) for i, j in pairs if 0 <= j < CONTEXT // ROWS])


def swapped(block):
    return permuted(block, [(i, i ^ 1) for i in range(DEVICES)])


def turned(block, distance):
    return permuted(block, [(i, (i + 32 * distance) % DEVICES) for i in range(DEVICES)])


HUBS = ((0, 3), (2, 3), (3, 0), (3, 2))
QUADRANTS = (
    ((0, 0), (0, 1), (0, 2), (0, 3)),
    ((2, 0), (2, 1), (2, 2), (2, 3)),
    ((3, 0), (3, 1), (1, 0), (1, 1)),
    ((3, 2), (3, 3), (1, 2), (1, 3)),
)


def in_ring(ring, holder):
    return (ring[0] * 4 + ring[1]) * 8 + 4 + holder


def hub_pairs(j):
    return [(DEVICES - 4 + o, in_ring(HUBS[j], o)) for o in range(4)]


def spoke_pairs(d):
    pairs = []
    for hub, members in zip(HUBS, QUADRANTS):
        member = members[(members.index(hub) + d) % 4]
        pairs += [(in_ring(hub, o), in_ring(member, o)) for o in range(4)]
    return pairs


def back_to_front(pairs):
    return [(j, i) for i, j in pairs]


def exchanged(blocks, axes):
    return lax.all_to_all(blocks, axes, split_axis=0, concat_axis=0, tiled=True)


def merged(stats):
    parts = exchanged(jnp.broadcast_to(stats, (4,) + stats.shape), ("yh", "yl"))
    tops, totals, sums = jnp.split(parts, 3, axis=1)
    top = jnp.max(tops, axis=0)
    factor = jnp.exp2(tops - top)
    total = jnp.sum(totals * factor, axis=0)
    return jnp.concatenate([top + jnp.log2(total), jnp.sum(sums * factor, axis=0) / total])


def added(*terms):
    return sum(t.astype(F32) for t in terms)


def shards(q, k, v, g, span_lengths):
    place = lax.axis_index(AXES)
    place_arg = place.reshape(1).astype(jnp.int32)
    last = place >= DEVICES - 4
    even = place % 2 == 0
    even_x = place // 32 % 2 == 0
    wide = GROUP * HEAD_WIDTH
    barrier = lax.optimization_barrier

    def headed(a):
        return a.reshape(ROWS, KEY_VALUE_HEADS, HEAD_WIDTH).transpose(1, 0, 2)

    kv = jnp.stack([headed(k), headed(v)], axis=1)
    same1 = shifted(kv, 2)
    same2 = shifted(same1, 2)
    blocks = (kv, same1, same2, swapped(kv), swapped(same1), swapped(same2))
    kv_ring = exchanged(kv, ("z", "c"))
    kv_ring = jnp.stack([kv_ring] + [turned(kv_ring, i) for i in (1, 2, 3)])

    def piece(a, j):
        return a[32 * j : 32 * j + 32].reshape(4, 8, -1)

    at_hub = sum(
        permuted(jnp.stack([piece(q, j), piece(g, j)], axis=1), hub_pairs(j)) for j in range(4)
    )
    at_hub, blocks = barrier((at_hub, blocks))

    def spoke(d):
        return lax.dynamic_index_in_dim(at_hub, jnp.where(even_x, (3 + d) % 4, d), 0, False)

    at_ring = [spoke(0)] + [permuted(spoke(d), spoke_pairs(d)) for d in (1, 2, 3)]
    context = context_attention(0, 3, place_arg, span_lengths, q, g, blocks)
    at_ring, context = barrier((at_ring, context))
    deal = sum(at_ring).reshape(2, 8, KEY_VALUE_HEADS, wide).transpose(2, 0, 1, 3)
    deal = exchanged(deal, ("z", "c"))
    context = context_attention(3, 3, place_arg, span_lengths, q, g, blocks, context)
    deal, context = barrier((deal, context))
    own = jnp.broadcast_to(deal[4:, None], (4, 4, 2, 8, wide))
    qg = exchanged(own.reshape(16, 2, 8, wide), PLANE)
    context = context_attention(6, 2, place_arg, span_lengths, q, g, blocks, context)
    qg, kv_ring, context = barrier((qg, kv_ring, context))
    out, dq, d0, d1, d2, d3, d4 = context

    stats = question_statistics(place_arg, qg, kv_ring)
    stats, from1, from3 = barrier((stats, swapped(d1), swapped(d3)))
    none = jnp.zeros_like(d1)
    far = shifted(added(d4, jnp.where(even, none, from3)).astype(BF16), -2)
    stats, far = barrier((merged(stats), far))
    near = shifted(added(d2, jnp.where(even, from3, from1), far).astype(BF16), -2)
    parts, dkv_ring = question_attention(place_arg, qg, kv_ring, stats)
    parts, dkv_ring, near = barrier((parts, dkv_ring, near))

    parts, dkv_ring = barrier((exchanged(parts, PLANE), dkv_ring))
    dkv_ring = added(dkv_ring[0], *[turned(dkv_ring[i], -i) for i in (1, 2, 3)])
    dkv_ring = exchanged(dkv_ring.astype(BF16), ("z", "c"))
    dkv = added(d0, jnp.where(even, from1, none), near, dkv_ring).astype(BF16)
    dk = dkv[:, 0].transpose(1, 0, 2).reshape(k.shape)
    dv = dkv[:, 1].transpose(1, 0, 2).reshape(v.shape)

    parts = jnp.sum(parts.reshape(4, 4, 2, 8, wide).astype(F32), axis=1).astype(BF16)
    parts = exchanged(jnp.concatenate([jnp.zeros_like(parts), parts]), ("z", "c"))
    mine = parts.transpose(1, 2, 0, 3).reshape(2, 8, KEY_VALUE_HEADS * wide)
    gathered = [permuted(mine, back_to_front(spoke_pairs(d))) for d in (1, 2, 3)]
    hub = jnp.where(even_x, jnp.stack(gathered + [mine]), jnp.stack([mine] + gathered))
    back = [permuted(hub, back_to_front(hub_pairs(j))) for j in range(4)]

    def result(which, context_rows):
        rows = jnp.concatenate([b[:, which].reshape(32, -1) for b in back])
        return jnp.where(last, rows, context_rows)

    return result(0, out), result(1, dq), dk, dv


def solution(mesh):
    grid = Mesh(mesh.devices.reshape(2, 4, 2, 4, 2), MESH_AXES)
    rows = P(AXES, None)
    return jax.shard_map(
        shards,
        mesh=grid,
        in_specs=(rows, rows, rows, rows, P()),
        out_specs=(rows,) * 4,
        check_vma=False,
    )
```

```python
import math

import jax
import jax.numpy as jnp
from jax import lax
from jax.experimental import pallas as pl
from jax.experimental.pallas import tpu as pltpu
from jax.sharding import Mesh
from jax.sharding import PartitionSpec as P

QUERY_HEADS = 64
KEY_VALUE_HEADS = 8
HEAD_WIDTH = 128
GROUP = QUERY_HEADS // KEY_VALUE_HEADS
QLEN = 512
ROWS = 128
BACK = 4
SPANS = 62
AXES = ("x", "yh", "yl", "z", "c")
MESH_AXES = ("yl", "z", "c", "x", "yh")
PLANE = ("x", "yh", "yl")
DEVICES = 128
CONTEXT = DEVICES * ROWS - QLEN
RING = 8 * ROWS
SCALE = 1.0 / math.sqrt(HEAD_WIDTH)
SCALE2 = SCALE * math.log2(math.e)
HIDDEN = -1e30
FLOOR = -1e29
BF16 = jnp.bfloat16
F32 = jnp.float32


def dot_nt(a, b):
    return lax.dot_general(a, b, (((1,), (1,)), ((), ())), preferred_element_type=F32)


def dot_nn(a, b):
    return lax.dot_general(a, b, (((1,), (0,)), ((), ())), preferred_element_type=F32)


def stacked(pair):
    return jnp.concatenate([pair[:, :HEAD_WIDTH], pair[:, HEAD_WIDTH:]], axis=0)


def unstacked(transposed):
    rows = transposed.T
    return jnp.concatenate([rows[:ROWS], rows[ROWS:]], axis=1).astype(BF16)


def context_kernel(
    place_ref, span_ref, q_ref, g_ref, same0, same1, same2, swapped0, swapped1, swapped2, *rest,
):
    rest = rest[-14:]
    out_ref, dq_ref, d0, d1, d2, d3, d4, bias, k_win, v_win, k_t, v_t, dk_acc, dv_acc = rest
    window = (BACK + 1) * ROWS
    group, pair = pl.program_id(0), pl.program_id(1)
    place = place_ref[0]

    @pl.when((group == 0) & (pair == 0))
    def _():
        row = place * ROWS + lax.broadcasted_iota(jnp.int32, (1, ROWS), 1)

        def step(n, carry):
            begin, start = carry
            start = jnp.where(row >= begin, begin, start)
            return begin + span_ref[n], start

        _, start = lax.fori_loop(0, SPANS, step, (jnp.int32(0), jnp.zeros((1, ROWS), jnp.int32)))
        start = jnp.where(row >= CONTEXT, DEVICES * ROWS, start)
        key = (place - BACK) * ROWS + lax.broadcasted_iota(jnp.int32, (window, ROWS), 0)
        bias[...] = jnp.where((key >= start) & (key <= row), 0.0, HIDDEN)

    def fill(i, ref):
        k_win[i * ROWS : (i + 1) * ROWS] = ref[0, 0]
        v_win[i * ROWS : (i + 1) * ROWS] = ref[0, 1]
        k_t[:, i * ROWS : (i + 1) * ROWS] = ref[0, 0].T
        v_t[:, i * ROWS : (i + 1) * ROWS] = ref[0, 1].T

    @pl.when(pair == 0)
    def _():
        fill(0, same2)
        fill(2, same1)
        fill(4, same0)
        dk_acc[...] = jnp.zeros_like(dk_acc)
        dv_acc[...] = jnp.zeros_like(dv_acc)

    @pl.when((pair == 0) & (place % 2 == 0))
    def _():
        fill(1, swapped2)
        fill(3, swapped1)

    @pl.when((pair == 0) & (place % 2 == 1))
    def _():
        fill(1, swapped1)
        fill(3, swapped0)

    q = stacked(q_ref[...])
    g = stacked(g_ref[...])
    hide = jnp.concatenate([bias[...], bias[...]], axis=1)
    s = dot_nt(k_win[...], q) * SCALE2 + hide
    top = jnp.maximum(jnp.max(s, axis=0, keepdims=True), FLOOR)
    w = jnp.exp2(s - top)
    total = jnp.sum(w, axis=0, keepdims=True)
    p = w * jnp.where(total > 0.0, 1.0 / total, 0.0)
    dp = dot_nt(v_win[...], g)
    dd = jnp.sum(p * dp, axis=0, keepdims=True)
    ds = (p * (dp - dd)).astype(BF16)
    pb = p.astype(BF16)
    out_ref[...] = unstacked(dot_nn(v_t[...], pb))
    dq_ref[...] = unstacked(dot_nn(k_t[...], ds) * SCALE)
    dv_acc[...] += dot_nn(pb, g)
    dk_acc[...] += dot_nn(ds, q)

    @pl.when(pair == GROUP // 2 - 1)
    def _():
        for i, ref in enumerate((d4, d3, d2, d1, d0)):
            ref[0, 0] = (dk_acc[i * ROWS : (i + 1) * ROWS] * SCALE).astype(BF16)
            ref[0, 1] = dv_acc[i * ROWS : (i + 1) * ROWS].astype(BF16)


def context_attention(first, count, place, span_lengths, q, g, blocks, before=()):
    window = (BACK + 1) * ROWS
    wide = pl.BlockSpec((ROWS, 2 * HEAD_WIDTH), lambda a, b, *_: (0, (a + first) * (GROUP // 2) + b))
    block = pl.BlockSpec((1, 2, ROWS, HEAD_WIDTH), lambda a, b, *_: (a + first, 0, 0, 0))
    whole = jax.ShapeDtypeStruct(q.shape, BF16)
    part = jax.ShapeDtypeStruct((KEY_VALUE_HEADS, 2, ROWS, HEAD_WIDTH), BF16)
    return pl.pallas_call(
        context_kernel,
        grid_spec=pltpu.PrefetchScalarGridSpec(
            num_scalar_prefetch=2,
            grid=(count, GROUP // 2),
            in_specs=[wide, wide] + [block] * 6 + [pl.BlockSpec(memory_space=pl.ANY)] * len(before),
            out_specs=[wide, wide] + [block] * 5,
            scratch_shapes=[
                pltpu.VMEM((window, ROWS), F32),
                pltpu.VMEM((window, HEAD_WIDTH), BF16),
                pltpu.VMEM((window, HEAD_WIDTH), BF16),
                pltpu.VMEM((HEAD_WIDTH, window), BF16),
                pltpu.VMEM((HEAD_WIDTH, window), BF16),
                pltpu.VMEM((window, HEAD_WIDTH), F32),
                pltpu.VMEM((window, HEAD_WIDTH), F32),
            ],
        ),
        out_shape=[whole, whole] + [part] * 5,
        input_output_aliases={10 + i: i for i in range(len(before))},
        name="context_rows",
    )(place, span_lengths, q, g, *blocks, *before)


def question_scores(place_ref, ring, k, q):
    s = dot_nt(k, q) * SCALE2
    lane = lax.broadcasted_iota(jnp.int32, (1, 2 * ROWS), 1) % ROWS
    x, y = lane // 32, lane // 8 % 4
    piece = jnp.where(x % 2 == 0, x * 2 + y, 8 + y // 2 * 4 + y % 2 + (3 - x))
    row = CONTEXT + place_ref[0] // 32 * ROWS + piece * 8 + lane % 8
    key = ring_of(place_ref[0], ring) * RING + lax.broadcasted_iota(jnp.int32, s.shape, 0)
    return jnp.where(key <= row, s, HIDDEN)


def ring_of(place, ring):
    return (place // 32 + 4 - ring) % 4 * 4 + place // 8 % 4


def question_pair(qg_ref, which):
    return stacked(qg_ref[:, which].reshape(ROWS, 2 * HEAD_WIDTH))


def ring_keys(kv_ref):
    return kv_ref[0, :, 0].reshape(RING, HEAD_WIDTH), kv_ref[0, :, 1].reshape(RING, HEAD_WIDTH)


def statistics_kernel(place_ref, qg_ref, kv_ref, stats_ref):
    pair, ring = pl.program_id(0), pl.program_id(1)
    k, v = ring_keys(kv_ref)
    q = question_pair(qg_ref, 0)
    g = question_pair(qg_ref, 1)
    s = question_scores(place_ref, ring, k, q)
    slots = [pl.ds(pl.multiple_of(part * GROUP, GROUP) + pair, 1) for part in range(3)]

    @pl.when(ring == 0)
    def _():
        stats_ref[slots[0], :] = jnp.full((1, 2 * ROWS), FLOOR, F32)
        stats_ref[slots[1], :] = jnp.zeros((1, 2 * ROWS), F32)
        stats_ref[slots[2], :] = jnp.zeros((1, 2 * ROWS), F32)

    before = stats_ref[slots[0], :]
    top = jnp.maximum(before, jnp.max(s, axis=0, keepdims=True))
    factor = jnp.exp2(before - top)
    w = jnp.exp2(s - top)
    stats_ref[slots[0], :] = top
    stats_ref[slots[1], :] = stats_ref[slots[1], :] * factor + jnp.sum(w, axis=0, keepdims=True)
    dd = jnp.sum(w * dot_nt(v, g), axis=0, keepdims=True)
    stats_ref[slots[2], :] = stats_ref[slots[2], :] * factor + dd


def question_kernel(
    place_ref, qg_ref, kv_ref, stats_ref, part_ref, dkv_ref, k_t, v_t, dk_acc, dv_acc, out_acc, dq_acc
):
    ring, pair = pl.program_id(0), pl.program_id(1)
    k, v = ring_keys(kv_ref)

    @pl.when(pair == 0)
    def _():
        k_t[...] = k.T
        v_t[...] = v.T
        dk_acc[...] = jnp.zeros_like(dk_acc)
        dv_acc[...] = jnp.zeros_like(dv_acc)

    @pl.when(ring == 0)
    def _():
        out_acc[pair] = jnp.zeros((HEAD_WIDTH, 2 * ROWS), F32)
        dq_acc[pair] = jnp.zeros((HEAD_WIDTH, 2 * ROWS), F32)

    q = question_pair(qg_ref, 0)
    g = question_pair(qg_ref, 1)
    s = question_scores(place_ref, ring, k, q)
    lse = stats_ref[pl.ds(pair, 1), :]
    dd = stats_ref[pl.ds(GROUP + pair, 1), :]
    p = jnp.exp2(s - lse)
    ds = (p * (dot_nt(v, g) - dd)).astype(BF16)
    pb = p.astype(BF16)
    out_acc[pair] += dot_nn(v_t[...], pb)
    dq_acc[pair] += dot_nn(k_t[...], ds)
    dv_acc[...] += dot_nn(pb, g)
    dk_acc[...] += dot_nn(ds, q)

    @pl.when(ring == 3)
    def _():
        shape = (16, 8, 2 * HEAD_WIDTH)
        part_ref[:, 0] = unstacked(out_acc[pair]).reshape(shape)
        part_ref[:, 1] = unstacked(dq_acc[pair] * SCALE).reshape(shape)

    @pl.when(pair == GROUP // 2 - 1)
    def _():
        dkv_ref[0, :, 0] = (dk_acc[...] * SCALE).astype(BF16).reshape(8, ROWS, HEAD_WIDTH)
        dkv_ref[0, :, 1] = dv_acc[...].astype(BF16).reshape(8, ROWS, HEAD_WIDTH)


def question_statistics(place, qg, kv):
    return pl.pallas_call(
        statistics_kernel,
        grid_spec=pltpu.PrefetchScalarGridSpec(
            num_scalar_prefetch=1,
            grid=(GROUP // 2, 4),
            in_specs=[
                pl.BlockSpec((16, 2, 8, 2 * HEAD_WIDTH), lambda h, r, *_: (0, 0, 0, h)),
                pl.BlockSpec((1, 8, 2, ROWS, HEAD_WIDTH), lambda h, r, *_: (r, 0, 0, 0, 0)),
            ],
            out_specs=pl.BlockSpec((3 * GROUP, 2 * ROWS), lambda h, r, *_: (0, 0)),
        ),
        out_shape=jax.ShapeDtypeStruct((3 * GROUP, 2 * ROWS), F32),
        name="question_statistics",
    )(place, qg, kv)


def question_attention(place, qg, kv, stats):
    rows = pl.BlockSpec((16, 2, 8, 2 * HEAD_WIDTH), lambda r, h, *_: (0, 0, 0, h))
    keys = pl.BlockSpec((1, 8, 2, ROWS, HEAD_WIDTH), lambda r, h, *_: (r, 0, 0, 0, 0))
    last_rows = pl.BlockSpec(
        (16, 2, 8, 2 * HEAD_WIDTH), lambda r, h, *_: (0, 0, 0, jnp.where(r == 3, h, 0))
    )
    return pl.pallas_call(
        question_kernel,
        grid_spec=pltpu.PrefetchScalarGridSpec(
            num_scalar_prefetch=1,
            grid=(4, GROUP // 2),
            in_specs=[rows, keys, pl.BlockSpec((2 * GROUP, 2 * ROWS), lambda r, h, *_: (0, 0))],
            out_specs=[last_rows, keys],
            scratch_shapes=[
                pltpu.VMEM((HEAD_WIDTH, RING), BF16),
                pltpu.VMEM((HEAD_WIDTH, RING), BF16),
                pltpu.VMEM((RING, HEAD_WIDTH), F32),
                pltpu.VMEM((RING, HEAD_WIDTH), F32),
                pltpu.VMEM((GROUP // 2, HEAD_WIDTH, 2 * ROWS), F32),
                pltpu.VMEM((GROUP // 2, HEAD_WIDTH, 2 * ROWS), F32),
            ],
        ),
        out_shape=[
            jax.ShapeDtypeStruct(qg.shape, BF16),
            jax.ShapeDtypeStruct(kv.shape, BF16),
        ],
        name="question_rows",
    )(place, qg, kv, stats)


def results_kernel(place_ref, out_in, dq_in, b0, b1, b2, b3, out_ref, dq_ref, done):
    @pl.when(place_ref[0] >= CONTEXT // ROWS)
    def _():
        copies = []
        for j, back in enumerate((b0, b1, b2, b3)):
            for t in range(4):
                for which, ref in enumerate((out_ref, dq_ref)):
                    copies.append(
                        pltpu.make_async_copy(
                            back.at[t, which],
                            ref.at[pl.ds(32 * j + 8 * t, 8)],
                            done.at[8 * j + 2 * t + which],
                        )
                    )
        for copy in copies:
            copy.start()
        for copy in copies:
            copy.wait()


def question_results(place, out, dq, back):
    anywhere = pl.BlockSpec(memory_space=pl.ANY)
    return pl.pallas_call(
        results_kernel,
        grid_spec=pltpu.PrefetchScalarGridSpec(
            num_scalar_prefetch=1,
            grid=(1,),
            in_specs=[anywhere] * 6,
            out_specs=[anywhere] * 2,
            scratch_shapes=[pltpu.SemaphoreType.DMA((32,))],
        ),
        out_shape=[jax.ShapeDtypeStruct(out.shape, BF16)] * 2,
        input_output_aliases={1: 0, 2: 1},
        name="question_results",
    )(place, out, dq, *back)


def permuted(block, pairs):
    index = [place % 16 * 8 + place // 16 for place in range(DEVICES)]
    return lax.ppermute(block, MESH_AXES, [(index[i], index[j]) for i, j in pairs])


def shifted(block, distance):
    pairs = [(i, i + distance) for i in range(CONTEXT // ROWS)]
    return permuted(block, [(i, j) for i, j in pairs if 0 <= j < CONTEXT // ROWS])


def swapped(block):
    return permuted(block, [(i, i ^ 1) for i in range(DEVICES)])


def turned(block, distance):
    return permuted(block, [(i, (i + 32 * distance) % DEVICES) for i in range(DEVICES)])


HUBS = ((0, 3), (2, 3), (3, 0), (3, 2))
QUADRANTS = (
    ((0, 0), (0, 1), (0, 2), (0, 3)),
    ((2, 0), (2, 1), (2, 2), (2, 3)),
    ((3, 0), (3, 1), (1, 0), (1, 1)),
    ((3, 2), (3, 3), (1, 2), (1, 3)),
)


def in_ring(ring, holder):
    return (ring[0] * 4 + ring[1]) * 8 + 4 + holder


def hub_pairs(j):
    return [(DEVICES - 4 + o, in_ring(HUBS[j], o)) for o in range(4)]


def spoke_pairs(d):
    pairs = []
    for hub, members in zip(HUBS, QUADRANTS):
        member = members[(members.index(hub) + d) % 4]
        pairs += [(in_ring(hub, o), in_ring(member, o)) for o in range(4)]
    return pairs


def back_to_front(pairs):
    return [(j, i) for i, j in pairs]


def exchanged(blocks, axes):
    return lax.all_to_all(blocks, axes, split_axis=0, concat_axis=0, tiled=True)


def merged(stats):
    parts = exchanged(jnp.broadcast_to(stats, (4,) + stats.shape), ("yh", "yl"))
    tops, totals, sums = jnp.split(parts, 3, axis=1)
    top = jnp.max(tops, axis=0)
    factor = jnp.exp2(tops - top)
    total = jnp.sum(totals * factor, axis=0)
    return jnp.concatenate([top + jnp.log2(total), jnp.sum(sums * factor, axis=0) / total])


def added(*terms):
    return sum(t.astype(F32) for t in terms)


def shards(q, k, v, g, span_lengths):
    place = lax.axis_index(AXES)
    place_arg = place.reshape(1).astype(jnp.int32)
    last = place >= DEVICES - 4
    even = place % 2 == 0
    even_x = place // 32 % 2 == 0
    wide = GROUP * HEAD_WIDTH
    barrier = lax.optimization_barrier

    def headed(a):
        return a.reshape(ROWS, KEY_VALUE_HEADS, HEAD_WIDTH).transpose(1, 0, 2)

    kv = jnp.stack([headed(k), headed(v)], axis=1)
    kv, q, g = barrier((kv, q, g))
    same1 = shifted(kv, 2)
    same2 = shifted(same1, 2)
    blocks = (kv, same1, same2, swapped(kv), swapped(same1), swapped(same2))
    kv_ring = exchanged(kv, ("z", "c"))

    def piece(a, j):
        return a[32 * j : 32 * j + 32].reshape(4, 8, -1)

    at_hub = sum(
        permuted(jnp.stack([piece(q, j), piece(g, j)], axis=1), hub_pairs(j)) for j in range(4)
    )
    at_hub, blocks, kv_ring = barrier((at_hub, blocks, kv_ring))
    kv_ring = [kv_ring] + [turned(kv_ring, i) for i in (1, 2, 3)]

    def spoke(d):
        return lax.dynamic_index_in_dim(at_hub, jnp.where(even_x, (3 + d) % 4, d), 0, False)

    at_ring = [spoke(0)] + [permuted(spoke(d), spoke_pairs(d)) for d in (1, 2, 3)]
    context = context_attention(0, 3, place_arg, span_lengths, q, g, blocks)
    at_ring, context = barrier((at_ring, context))
    deal = sum(at_ring).reshape(2, 8, KEY_VALUE_HEADS, wide).transpose(2, 0, 1, 3)
    deal = exchanged(deal, ("z", "c"))
    context = context_attention(3, 3, place_arg, span_lengths, q, g, blocks, context)
    deal, context = barrier((deal, context))
    own = jnp.broadcast_to(deal[4:, None], (4, 4, 2, 8, wide))
    qg = exchanged(own.reshape(16, 2, 8, wide), PLANE)
    context = context_attention(6, 2, place_arg, span_lengths, q, g, blocks, context)
    qg, kv_ring, context = barrier((qg, jnp.stack(kv_ring), context))
    out, dq, d0, d1, d2, d3, d4 = context

    stats = question_statistics(place_arg, qg, kv_ring)
    stats, from1, from3 = barrier((stats, swapped(d1), swapped(d3)))
    none = jnp.zeros_like(d1)
    far = shifted(added(d4, jnp.where(even, none, from3)).astype(BF16), -2)
    parts, dkv_ring = question_attention(place_arg, qg, kv_ring, merged(stats))
    parts, dkv_ring, far = barrier((parts, dkv_ring, far))
    near = shifted(added(d2, jnp.where(even, from3, from1), far).astype(BF16), -2)

    parts = exchanged(parts, PLANE)
    parts = jnp.sum(parts.reshape(4, 4, 2, 8, wide).astype(F32), axis=1).astype(BF16)
    parts = exchanged(jnp.concatenate([jnp.zeros_like(parts), parts]), ("z", "c"))
    parts, dkv_ring = barrier((parts, dkv_ring))
    mine = parts.transpose(1, 2, 0, 3).reshape(2, 8, KEY_VALUE_HEADS * wide)
    gathered = [permuted(mine, back_to_front(spoke_pairs(d))) for d in (1, 2, 3)]
    hub = jnp.where(even_x, jnp.stack(gathered + [mine]), jnp.stack([mine] + gathered))
    back = [permuted(hub, back_to_front(hub_pairs(j))) for j in range(4)]

    dkv_ring = added(dkv_ring[0], *[turned(dkv_ring[i], -i) for i in (1, 2, 3)])
    dkv_ring = exchanged(dkv_ring.astype(BF16), ("z", "c"))
    dkv = added(d0, jnp.where(even, from1, none), near, dkv_ring).astype(BF16)
    dk = dkv[:, 0].transpose(1, 0, 2).reshape(k.shape)
    dv = dkv[:, 1].transpose(1, 0, 2).reshape(v.shape)

    out, dq = question_results(place_arg, out, dq, back)
    return out, dq, dk, dv


def solution(mesh):
    grid = Mesh(mesh.devices.reshape(2, 4, 2, 4, 2), MESH_AXES)
    rows = P(AXES, None)
    return jax.shard_map(
        shards,
        mesh=grid,
        in_specs=(rows, rows, rows, rows, P()),
        out_specs=(rows,) * 4,
        check_vma=False,
    )
```

```python
import math

import jax
import jax.numpy as jnp
from jax import lax
from jax.experimental import pallas as pl
from jax.experimental.pallas import tpu as pltpu
from jax.sharding import Mesh
from jax.sharding import PartitionSpec as P

QUERY_HEADS = 64
KEY_VALUE_HEADS = 8
HEAD_WIDTH = 128
GROUP = QUERY_HEADS // KEY_VALUE_HEADS
QLEN = 512
ROWS = 128
BACK = 4
SPANS = 62
AXES = ("x", "yh", "yl", "z", "c")
MESH_AXES = ("yl", "z", "c", "x", "yh")
PLANE = ("x", "yh", "yl")
DEVICES = 128
CONTEXT = DEVICES * ROWS - QLEN
RING = 8 * ROWS
SCALE = 1.0 / math.sqrt(HEAD_WIDTH)
SCALE2 = SCALE * math.log2(math.e)
HIDDEN = -1e30
FLOOR = -1e29
BF16 = jnp.bfloat16
F32 = jnp.float32


HUBS = ((0, 3), (2, 3), (3, 0), (3, 2))
QUADRANTS = (
    ((0, 0), (0, 1), (0, 2), (0, 3)),
    ((2, 0), (2, 1), (2, 2), (2, 3)),
    ((3, 0), (3, 1), (1, 0), (1, 1)),
    ((3, 2), (3, 3), (1, 2), (1, 3)),
)


def dot_nt(a, b):
    return lax.dot_general(a, b, (((1,), (1,)), ((), ())), preferred_element_type=F32)


def dot_nn(a, b):
    return lax.dot_general(a, b, (((1,), (0,)), ((), ())), preferred_element_type=F32)


def stacked(pair):
    return jnp.concatenate([pair[:, :HEAD_WIDTH], pair[:, HEAD_WIDTH:]], axis=0)


def unstacked(transposed):
    rows = transposed.T
    return jnp.concatenate([rows[:ROWS], rows[ROWS:]], axis=1).astype(BF16)


def context_kernel(
    place_ref, span_ref, q_ref, g_ref, same0, same1, same2, swapped0, swapped1, swapped2, *rest,
):
    rest = rest[-14:]
    out_ref, dq_ref, d0, d1, d2, d3, d4, bias, k_win, v_win, k_t, v_t, dk_acc, dv_acc = rest
    window = (BACK + 1) * ROWS
    group, pair = pl.program_id(0), pl.program_id(1)
    place = place_ref[0]

    @pl.when((group == 0) & (pair == 0))
    def _():
        row = place * ROWS + lax.broadcasted_iota(jnp.int32, (1, ROWS), 1)

        def step(n, carry):
            begin, start = carry
            start = jnp.where(row >= begin, begin, start)
            return begin + span_ref[n], start

        _, start = lax.fori_loop(0, SPANS, step, (jnp.int32(0), jnp.zeros((1, ROWS), jnp.int32)))
        start = jnp.where(row >= CONTEXT, DEVICES * ROWS, start)
        key = (place - BACK) * ROWS + lax.broadcasted_iota(jnp.int32, (window, ROWS), 0)
        bias[...] = jnp.where((key >= start) & (key <= row), 0.0, HIDDEN)

    def fill(i, ref):
        k_win[i * ROWS : (i + 1) * ROWS] = ref[0, 0]
        v_win[i * ROWS : (i + 1) * ROWS] = ref[0, 1]
        k_t[:, i * ROWS : (i + 1) * ROWS] = ref[0, 0].T
        v_t[:, i * ROWS : (i + 1) * ROWS] = ref[0, 1].T

    @pl.when(pair == 0)
    def _():
        fill(0, same2)
        fill(2, same1)
        fill(4, same0)
        dk_acc[...] = jnp.zeros_like(dk_acc)
        dv_acc[...] = jnp.zeros_like(dv_acc)

    @pl.when((pair == 0) & (place % 2 == 0))
    def _():
        fill(1, swapped2)
        fill(3, swapped1)

    @pl.when((pair == 0) & (place % 2 == 1))
    def _():
        fill(1, swapped1)
        fill(3, swapped0)

    q = stacked(q_ref[...])
    g = stacked(g_ref[...])
    hide = jnp.concatenate([bias[...], bias[...]], axis=1)
    s = dot_nt(k_win[...], q) * SCALE2 + hide
    top = jnp.maximum(jnp.max(s, axis=0, keepdims=True), FLOOR)
    w = jnp.exp2(s - top)
    total = jnp.sum(w, axis=0, keepdims=True)
    p = w * jnp.where(total > 0.0, 1.0 / total, 0.0)
    dp = dot_nt(v_win[...], g)
    dd = jnp.sum(p * dp, axis=0, keepdims=True)
    ds = (p * (dp - dd)).astype(BF16)
    pb = p.astype(BF16)
    out_ref[...] = unstacked(dot_nn(v_t[...], pb))
    dq_ref[...] = unstacked(dot_nn(k_t[...], ds) * SCALE)
    dv_acc[...] += dot_nn(pb, g)
    dk_acc[...] += dot_nn(ds, q)

    @pl.when(pair == GROUP // 2 - 1)
    def _():
        for i, ref in enumerate((d4, d3, d2, d1, d0)):
            ref[0, 0] = (dk_acc[i * ROWS : (i + 1) * ROWS] * SCALE).astype(BF16)
            ref[0, 1] = dv_acc[i * ROWS : (i + 1) * ROWS].astype(BF16)


def context_attention(first, count, place, span_lengths, q, g, blocks, before=()):
    window = (BACK + 1) * ROWS
    wide = pl.BlockSpec((ROWS, 2 * HEAD_WIDTH), lambda a, b, *_: (0, (a + first) * (GROUP // 2) + b))
    block = pl.BlockSpec((1, 2, ROWS, HEAD_WIDTH), lambda a, b, *_: (a + first, 0, 0, 0))
    whole = jax.ShapeDtypeStruct(q.shape, BF16)
    part = jax.ShapeDtypeStruct((KEY_VALUE_HEADS, 2, ROWS, HEAD_WIDTH), BF16)
    return pl.pallas_call(
        context_kernel,
        grid_spec=pltpu.PrefetchScalarGridSpec(
            num_scalar_prefetch=2,
            grid=(count, GROUP // 2),
            in_specs=[wide, wide] + [block] * 6 + [pl.BlockSpec(memory_space=pl.ANY)] * len(before),
            out_specs=[wide, wide] + [block] * 5,
            scratch_shapes=[
                pltpu.VMEM((window, ROWS), F32),
                pltpu.VMEM((window, HEAD_WIDTH), BF16),
                pltpu.VMEM((window, HEAD_WIDTH), BF16),
                pltpu.VMEM((HEAD_WIDTH, window), BF16),
                pltpu.VMEM((HEAD_WIDTH, window), BF16),
                pltpu.VMEM((window, HEAD_WIDTH), F32),
                pltpu.VMEM((window, HEAD_WIDTH), F32),
            ],
        ),
        out_shape=[whole, whole] + [part] * 5,
        input_output_aliases={10 + i: i for i in range(len(before))},
        name="context_rows",
    )(place, span_lengths, q, g, *blocks, *before)


def question_scores(place_ref, ring, k, q):
    s = dot_nt(k, q) * SCALE2
    lane = lax.broadcasted_iota(jnp.int32, (1, 2 * ROWS), 1) % ROWS
    x, y = lane // 32, lane // 8 % 4
    piece = jnp.where(x % 2 == 0, x * 2 + y, 8 + y // 2 * 4 + y % 2 + (3 - x))
    row = CONTEXT + place_ref[0] // 32 * ROWS + piece * 8 + lane % 8
    key = ring_of(place_ref[0], ring) * RING + lax.broadcasted_iota(jnp.int32, s.shape, 0)
    return jnp.where(key <= row, s, HIDDEN)


def ring_of(place, ring):
    return (place // 32 + 4 - ring) % 4 * 4 + place // 8 % 4


def question_pair(qg_ref, which):
    return stacked(qg_ref[:, which].reshape(ROWS, 2 * HEAD_WIDTH))


def ring_keys(kv_ref):
    return kv_ref[0, :, 0].reshape(RING, HEAD_WIDTH), kv_ref[0, :, 1].reshape(RING, HEAD_WIDTH)


def statistics_kernel(place_ref, qg_ref, kv_ref, stats_ref):
    pair, ring = pl.program_id(0), pl.program_id(1)
    k, v = ring_keys(kv_ref)
    q = question_pair(qg_ref, 0)
    g = question_pair(qg_ref, 1)
    s = question_scores(place_ref, ring, k, q)
    slots = [pl.ds(pl.multiple_of(part * GROUP, GROUP) + pair, 1) for part in range(3)]

    @pl.when(ring == 0)
    def _():
        stats_ref[slots[0], :] = jnp.full((1, 2 * ROWS), FLOOR, F32)
        stats_ref[slots[1], :] = jnp.zeros((1, 2 * ROWS), F32)
        stats_ref[slots[2], :] = jnp.zeros((1, 2 * ROWS), F32)

    before = stats_ref[slots[0], :]
    top = jnp.maximum(before, jnp.max(s, axis=0, keepdims=True))
    factor = jnp.exp2(before - top)
    w = jnp.exp2(s - top)
    stats_ref[slots[0], :] = top
    stats_ref[slots[1], :] = stats_ref[slots[1], :] * factor + jnp.sum(w, axis=0, keepdims=True)
    dd = jnp.sum(w * dot_nt(v, g), axis=0, keepdims=True)
    stats_ref[slots[2], :] = stats_ref[slots[2], :] * factor + dd


def question_kernel(
    place_ref, qg_ref, kv_ref, stats_ref, part_ref, dkv_ref, k_t, v_t, dk_acc, dv_acc, out_acc, dq_acc
):
    ring, pair = pl.program_id(0), pl.program_id(1)
    k, v = ring_keys(kv_ref)

    @pl.when(pair == 0)
    def _():
        k_t[...] = k.T
        v_t[...] = v.T
        dk_acc[...] = jnp.zeros_like(dk_acc)
        dv_acc[...] = jnp.zeros_like(dv_acc)

    @pl.when(ring == 0)
    def _():
        out_acc[pair] = jnp.zeros((HEAD_WIDTH, 2 * ROWS), F32)
        dq_acc[pair] = jnp.zeros((HEAD_WIDTH, 2 * ROWS), F32)

    q = question_pair(qg_ref, 0)
    g = question_pair(qg_ref, 1)
    s = question_scores(place_ref, ring, k, q)
    lse = stats_ref[pl.ds(pair, 1), :]
    dd = stats_ref[pl.ds(GROUP + pair, 1), :]
    p = jnp.exp2(s - lse)
    ds = (p * (dot_nt(v, g) - dd)).astype(BF16)
    pb = p.astype(BF16)
    out_acc[pair] += dot_nn(v_t[...], pb)
    dq_acc[pair] += dot_nn(k_t[...], ds)
    dv_acc[...] += dot_nn(pb, g)
    dk_acc[...] += dot_nn(ds, q)

    @pl.when(ring == 3)
    def _():
        shape = (16, 8, 2 * HEAD_WIDTH)
        part_ref[:, 0] = unstacked(out_acc[pair]).reshape(shape)
        part_ref[:, 1] = unstacked(dq_acc[pair] * SCALE).reshape(shape)

    @pl.when(pair == GROUP // 2 - 1)
    def _():
        dkv_ref[0, :, 0] = (dk_acc[...] * SCALE).astype(BF16).reshape(8, ROWS, HEAD_WIDTH)
        dkv_ref[0, :, 1] = dv_acc[...].astype(BF16).reshape(8, ROWS, HEAD_WIDTH)


def question_statistics(place, qg, kv):
    return pl.pallas_call(
        statistics_kernel,
        grid_spec=pltpu.PrefetchScalarGridSpec(
            num_scalar_prefetch=1,
            grid=(GROUP // 2, 4),
            in_specs=[
                pl.BlockSpec((16, 2, 8, 2 * HEAD_WIDTH), lambda h, r, *_: (0, 0, 0, h)),
                pl.BlockSpec((1, 8, 2, ROWS, HEAD_WIDTH), lambda h, r, *_: (r, 0, 0, 0, 0)),
            ],
            out_specs=pl.BlockSpec((3 * GROUP, 2 * ROWS), lambda h, r, *_: (0, 0)),
        ),
        out_shape=jax.ShapeDtypeStruct((3 * GROUP, 2 * ROWS), F32),
        name="question_statistics",
    )(place, qg, kv)


def question_attention(place, qg, kv, stats):
    rows = pl.BlockSpec((16, 2, 8, 2 * HEAD_WIDTH), lambda r, h, *_: (0, 0, 0, h))
    keys = pl.BlockSpec((1, 8, 2, ROWS, HEAD_WIDTH), lambda r, h, *_: (r, 0, 0, 0, 0))
    last_rows = pl.BlockSpec(
        (16, 2, 8, 2 * HEAD_WIDTH), lambda r, h, *_: (0, 0, 0, jnp.where(r == 3, h, 0))
    )
    return pl.pallas_call(
        question_kernel,
        grid_spec=pltpu.PrefetchScalarGridSpec(
            num_scalar_prefetch=1,
            grid=(4, GROUP // 2),
            in_specs=[rows, keys, pl.BlockSpec((2 * GROUP, 2 * ROWS), lambda r, h, *_: (0, 0))],
            out_specs=[last_rows, keys],
            scratch_shapes=[
                pltpu.VMEM((HEAD_WIDTH, RING), BF16),
                pltpu.VMEM((HEAD_WIDTH, RING), BF16),
                pltpu.VMEM((RING, HEAD_WIDTH), F32),
                pltpu.VMEM((RING, HEAD_WIDTH), F32),
                pltpu.VMEM((GROUP // 2, HEAD_WIDTH, 2 * ROWS), F32),
                pltpu.VMEM((GROUP // 2, HEAD_WIDTH, 2 * ROWS), F32),
            ],
        ),
        out_shape=[
            jax.ShapeDtypeStruct(qg.shape, BF16),
            jax.ShapeDtypeStruct(kv.shape, BF16),
        ],
        name="question_rows",
    )(place, qg, kv, stats)


def copied(sources, targets, done):
    for pairs in (sources, targets):
        copies = [pltpu.make_async_copy(a, b, done.at[i]) for i, (a, b) in enumerate(pairs)]
        for copy in copies:
            copy.start()
        for copy in copies:
            copy.wait()


def move_call(kernel, name, place, arrays, shapes, room, copies, aliases=None):
    anywhere = pl.BlockSpec(memory_space=pl.ANY)
    return pl.pallas_call(
        kernel,
        grid_spec=pltpu.PrefetchScalarGridSpec(
            num_scalar_prefetch=1,
            grid=(1,),
            in_specs=[anywhere] * len(arrays),
            out_specs=[anywhere] * len(shapes),
            scratch_shapes=[pltpu.VMEM(room, BF16), pltpu.SemaphoreType.DMA((copies,))],
        ),
        out_shape=[jax.ShapeDtypeStruct(shape, BF16) for shape in shapes],
        input_output_aliases=aliases or {},
        name=name,
    )(place, *arrays)


def pieces_kernel(place_ref, q_ref, g_ref, p0, p1, p2, p3, room, done):
    @pl.when(place_ref[0] >= CONTEXT // ROWS)
    def _():
        targets = []
        for j, piece in enumerate((p0, p1, p2, p3)):
            for t in range(4):
                for which in range(2):
                    rows = pl.ds(32 * j + 8 * t, 8)
                    targets.append((room.at[which, rows], piece.at[t, which]))
        copied([(q_ref, room.at[0]), (g_ref, room.at[1])], targets, done)


def question_pieces(place, q, g):
    width = q.shape[1]
    return move_call(
        pieces_kernel, "question_pieces", place, (q, g), [(4, 2, 8, width)] * 4, (2, ROWS, width), 32
    )


def spokes_kernel(place_ref, p0, p1, p2, p3, s0, s1, s2, s3, room, done):
    ring = place_ref[0] // 8
    for hub, piece, members in zip(HUBS, (p0, p1, p2, p3), QUADRANTS):

        @pl.when((ring == hub[0] * 4 + hub[1]) & (place_ref[0] % 8 >= 4))
        def _():
            first = members.index(hub)
            targets = [(room.at[(first + d) % 4], s) for d, s in enumerate((s0, s1, s2, s3))]
            copied([(piece, room)], targets, done)


def question_spokes(place, pieces):
    shape = pieces[0].shape
    return move_call(spokes_kernel, "question_spokes", place, pieces, [shape[1:]] * 4, shape, 4)


def pick_kernel(place_ref, s0, s1, s2, s3, deal_ref, room, done):
    x, y = place_ref[0] // 32, place_ref[0] // 8 % 4
    step = jnp.where(x % 2 == 0, (y + 1) % 4, y % 2 + 3 - x)
    wide = GROUP * HEAD_WIDTH
    for d, piece in enumerate((s0, s1, s2, s3)):

        @pl.when((step == d) & (place_ref[0] % 8 >= 4))
        def _():
            groups = range(KEY_VALUE_HEADS)
            targets = [(room.at[:, :, pl.ds(k * wide, wide)], deal_ref.at[k]) for k in groups]
            copied([(piece, room)], targets, done)


def question_pick(place, spokes):
    shape = spokes[0].shape
    deal = (KEY_VALUE_HEADS, 2, 8, GROUP * HEAD_WIDTH)
    return move_call(pick_kernel, "question_pick", place, spokes, [deal], shape, KEY_VALUE_HEADS)[0]


def results_kernel(place_ref, out_in, dq_in, b0, b1, b2, b3, out_ref, dq_ref, room, done):
    @pl.when(place_ref[0] >= CONTEXT // ROWS)
    def _():
        sources, targets = [], []
        for j, back in enumerate((b0, b1, b2, b3)):
            sources.append((back, room.at[j]))
            for t in range(4):
                for which, ref in enumerate((out_ref, dq_ref)):
                    rows = pl.ds(32 * j + 8 * t, 8)
                    targets.append((room.at[j, t, which], ref.at[rows]))
        copied(sources, targets, done)


def question_results(place, out, dq, back):
    return move_call(
        results_kernel, "question_results", place, (out, dq, *back), [out.shape] * 2,
        (4,) + back[0].shape, 32, {1: 0, 2: 1},
    )


def permuted(block, pairs):
    index = [place % 16 * 8 + place // 16 for place in range(DEVICES)]
    return lax.ppermute(block, MESH_AXES, [(index[i], index[j]) for i, j in pairs])


def shifted(block, distance):
    pairs = [(i, i + distance) for i in range(CONTEXT // ROWS)]
    return permuted(block, [(i, j) for i, j in pairs if 0 <= j < CONTEXT // ROWS])


def swapped(block):
    return permuted(block, [(i, i ^ 1) for i in range(DEVICES)])


def turned(block, distance):
    return permuted(block, [(i, (i + 32 * distance) % DEVICES) for i in range(DEVICES)])


def in_ring(ring, holder):
    return (ring[0] * 4 + ring[1]) * 8 + 4 + holder


def hub_pairs(j):
    return [(DEVICES - 4 + o, in_ring(HUBS[j], o)) for o in range(4)]


def spoke_pairs(d):
    pairs = []
    for hub, members in zip(HUBS, QUADRANTS):
        member = members[(members.index(hub) + d) % 4]
        pairs += [(in_ring(hub, o), in_ring(member, o)) for o in range(4)]
    return pairs


def back_to_front(pairs):
    return [(j, i) for i, j in pairs]


def exchanged(blocks, axes):
    return lax.all_to_all(blocks, axes, split_axis=0, concat_axis=0, tiled=True)


def merged(stats):
    parts = exchanged(jnp.broadcast_to(stats, (4,) + stats.shape), ("yh", "yl"))
    tops, totals, sums = jnp.split(parts, 3, axis=1)
    top = jnp.max(tops, axis=0)
    factor = jnp.exp2(tops - top)
    total = jnp.sum(totals * factor, axis=0)
    return jnp.concatenate([top + jnp.log2(total), jnp.sum(sums * factor, axis=0) / total])


def added(*terms):
    return sum(t.astype(F32) for t in terms)


def shards(q, k, v, g, span_lengths):
    place = lax.axis_index(AXES)
    place_arg = place.reshape(1).astype(jnp.int32)
    last = place >= DEVICES - 4
    even = place % 2 == 0
    even_x = place // 32 % 2 == 0
    wide = GROUP * HEAD_WIDTH
    barrier = lax.optimization_barrier

    def headed(a):
        return a.reshape(ROWS, KEY_VALUE_HEADS, HEAD_WIDTH).transpose(1, 0, 2)

    kv = jnp.stack([headed(k), headed(v)], axis=1)
    swap, q_tied, g_tied = barrier((swapped(kv), q, g))
    pieces = question_pieces(place_arg, q_tied, g_tied)
    same1, _ = barrier((shifted(kv, 2), pieces[0]))
    same2 = shifted(same1, 2)
    blocks = (kv, same1, same2, swap, swapped(same1), swapped(same2))
    kv_ring = exchanged(kv, ("z", "c"))

    pieces = [permuted(pieces[j], hub_pairs(j)) for j in range(4)]
    context = context_attention(0, 2, place_arg, span_lengths, q, g, blocks)
    pieces, kv_ring, context = barrier((pieces, kv_ring, context))
    kv_ring = [kv_ring] + [turned(kv_ring, i) for i in (1, 2, 3)]
    spokes = question_spokes(place_arg, pieces)
    spokes = [spokes[0]] + [permuted(spokes[d], spoke_pairs(d)) for d in (1, 2, 3)]
    context = context_attention(2, 2, place_arg, span_lengths, q, g, blocks, context)
    spokes, context = barrier((spokes, context))
    deal = exchanged(question_pick(place_arg, spokes), ("z", "c"))
    context = context_attention(4, 2, place_arg, span_lengths, q, g, blocks, context)
    deal, context = barrier((deal, context))
    own = jnp.broadcast_to(deal[4:, None], (4, 4, 2, 8, wide))
    qg = exchanged(own.reshape(16, 2, 8, wide), PLANE)
    context = context_attention(6, 2, place_arg, span_lengths, q, g, blocks, context)
    qg, kv_ring, context = barrier((qg, jnp.stack(kv_ring), context))
    out, dq, d0, d1, d2, d3, d4 = context

    stats = question_statistics(place_arg, qg, kv_ring)
    stats, from1, from3 = barrier((stats, swapped(d1), swapped(d3)))
    none = jnp.zeros_like(d1)
    far = shifted(added(d4, jnp.where(even, none, from3)).astype(BF16), -2)
    parts, dkv_ring = question_attention(place_arg, qg, kv_ring, merged(stats))
    parts, dkv_ring, far = barrier((parts, dkv_ring, far))
    near = shifted(added(d2, jnp.where(even, from3, from1), far).astype(BF16), -2)

    parts = exchanged(parts, PLANE)
    parts = jnp.sum(parts.reshape(4, 4, 2, 8, wide).astype(F32), axis=1).astype(BF16)
    parts = exchanged(jnp.concatenate([jnp.zeros_like(parts), parts]), ("z", "c"))
    parts, dkv_ring = barrier((parts, dkv_ring))
    mine = parts.transpose(1, 2, 0, 3).reshape(2, 8, KEY_VALUE_HEADS * wide)
    gathered = [permuted(mine, back_to_front(spoke_pairs(d))) for d in (1, 2, 3)]
    hub = jnp.where(even_x, jnp.stack(gathered + [mine]), jnp.stack([mine] + gathered))
    back = [permuted(hub, back_to_front(hub_pairs(j))) for j in range(4)]

    dkv_ring = added(dkv_ring[0], *[turned(dkv_ring[i], -i) for i in (1, 2, 3)])
    dkv_ring = exchanged(dkv_ring.astype(BF16), ("z", "c"))
    dkv = added(d0, jnp.where(even, from1, none), near, dkv_ring).astype(BF16)
    dk = dkv[:, 0].transpose(1, 0, 2).reshape(k.shape)
    dv = dkv[:, 1].transpose(1, 0, 2).reshape(v.shape)

    out, dq = question_results(place_arg, out, dq, back)
    return out, dq, dk, dv


def solution(mesh):
    grid = Mesh(mesh.devices.reshape(2, 4, 2, 4, 2), MESH_AXES)
    rows = P(AXES, None)
    return jax.shard_map(
        shards,
        mesh=grid,
        in_specs=(rows, rows, rows, rows, P()),
        out_specs=(rows,) * 4,
        check_vma=False,
    )
```

```python
import math

import jax
import jax.numpy as jnp
from jax import lax
from jax.experimental import pallas as pl
from jax.experimental.pallas import tpu as pltpu
from jax.sharding import Mesh
from jax.sharding import PartitionSpec as P


QUERY_HEADS = 64
KEY_VALUE_HEADS = 8
HEAD_WIDTH = 128
GROUP = QUERY_HEADS // KEY_VALUE_HEADS
QLEN = 512
ROWS = 128
BACK = 4
SPANS = 62
AXES = ("x", "yh", "yl", "z", "c")
MESH_AXES = ("yl", "z", "c", "x", "yh")
PLANE = ("x", "yh", "yl")
DEVICES = 128
CONTEXT = DEVICES * ROWS - QLEN
RING = 8 * ROWS
SCALE = 1.0 / math.sqrt(HEAD_WIDTH)
SCALE2 = SCALE * math.log2(math.e)
HIDDEN = -1e30
FLOOR = -1e29
BF16 = jnp.bfloat16
F32 = jnp.float32


HUBS = ((0, 3), (2, 3), (3, 0), (3, 2))
QUADRANTS = (
    ((0, 0), (0, 1), (0, 2), (0, 3)),
    ((2, 0), (2, 1), (2, 2), (2, 3)),
    ((3, 0), (3, 1), (1, 0), (1, 1)),
    ((3, 2), (3, 3), (1, 2), (1, 3)),
)


def dot_nt(a, b):
    return lax.dot_general(a, b, (((1,), (1,)), ((), ())), preferred_element_type=F32)


def dot_nn(a, b):
    return lax.dot_general(a, b, (((1,), (0,)), ((), ())), preferred_element_type=F32)


def stacked(pair):
    return jnp.concatenate([pair[:, :HEAD_WIDTH], pair[:, HEAD_WIDTH:]], axis=0)


def unstacked(transposed):
    rows = transposed.T
    return jnp.concatenate([rows[:ROWS], rows[ROWS:]], axis=1).astype(BF16)


def context_kernel(
    place_ref, span_ref, q_ref, g_ref, same0, same1, same2, swapped0, swapped1, swapped2, *rest,
):
    rest = rest[-14:]
    out_ref, dq_ref, d0, d1, d2, d3, d4, bias, k_win, v_win, k_t, v_t, dk_acc, dv_acc = rest
    window = (BACK + 1) * ROWS
    group, pair = pl.program_id(0), pl.program_id(1)
    place = place_ref[0]

    @pl.when((group == 0) & (pair == 0))
    def _():
        row = place * ROWS + lax.broadcasted_iota(jnp.int32, (1, ROWS), 1)

        def step(n, carry):
            begin, start = carry
            start = jnp.where(row >= begin, begin, start)
            return begin + span_ref[n], start

        _, start = lax.fori_loop(0, SPANS, step, (jnp.int32(0), jnp.zeros((1, ROWS), jnp.int32)))
        start = jnp.where(row >= CONTEXT, DEVICES * ROWS, start)
        key = (place - BACK) * ROWS + lax.broadcasted_iota(jnp.int32, (window, ROWS), 0)
        bias[...] = jnp.where((key >= start) & (key <= row), 0.0, HIDDEN)

    def fill(i, ref):
        k_win[i * ROWS : (i + 1) * ROWS] = ref[0, 0]
        v_win[i * ROWS : (i + 1) * ROWS] = ref[0, 1]
        k_t[:, i * ROWS : (i + 1) * ROWS] = ref[0, 0].T
        v_t[:, i * ROWS : (i + 1) * ROWS] = ref[0, 1].T

    @pl.when(pair == 0)
    def _():
        fill(0, same2)
        fill(2, same1)
        fill(4, same0)
        dk_acc[...] = jnp.zeros_like(dk_acc)
        dv_acc[...] = jnp.zeros_like(dv_acc)

    @pl.when((pair == 0) & (place % 2 == 0))
    def _():
        fill(1, swapped2)
        fill(3, swapped1)

    @pl.when((pair == 0) & (place % 2 == 1))
    def _():
        fill(1, swapped1)
        fill(3, swapped0)

    q = stacked(q_ref[...])
    g = stacked(g_ref[...])
    hide = jnp.concatenate([bias[...], bias[...]], axis=1)
    s = dot_nt(k_win[...], q) * SCALE2 + hide
    top = jnp.maximum(jnp.max(s, axis=0, keepdims=True), FLOOR)
    w = jnp.exp2(s - top)
    total = jnp.sum(w, axis=0, keepdims=True)
    p = w * jnp.where(total > 0.0, 1.0 / total, 0.0)
    dp = dot_nt(v_win[...], g)
    dd = jnp.sum(p * dp, axis=0, keepdims=True)
    ds = (p * (dp - dd)).astype(BF16)
    pb = p.astype(BF16)
    out_ref[...] = unstacked(dot_nn(v_t[...], pb))
    dq_ref[...] = unstacked(dot_nn(k_t[...], ds) * SCALE)
    dv_acc[...] += dot_nn(pb, g)
    dk_acc[...] += dot_nn(ds, q)

    @pl.when(pair == GROUP // 2 - 1)
    def _():
        for i, ref in enumerate((d4, d3, d2, d1, d0)):
            ref[0, 0] = (dk_acc[i * ROWS : (i + 1) * ROWS] * SCALE).astype(BF16)
            ref[0, 1] = dv_acc[i * ROWS : (i + 1) * ROWS].astype(BF16)


def context_attention(first, count, place, span_lengths, q, g, blocks, before=()):
    window = (BACK + 1) * ROWS
    wide = pl.BlockSpec((ROWS, 2 * HEAD_WIDTH), lambda a, b, *_: (0, (a + first) * (GROUP // 2) + b))
    block = pl.BlockSpec((1, 2, ROWS, HEAD_WIDTH), lambda a, b, *_: (a + first, 0, 0, 0))
    whole = jax.ShapeDtypeStruct(q.shape, BF16)
    part = jax.ShapeDtypeStruct((KEY_VALUE_HEADS, 2, ROWS, HEAD_WIDTH), BF16)
    return pl.pallas_call(
        context_kernel,
        grid_spec=pltpu.PrefetchScalarGridSpec(
            num_scalar_prefetch=2,
            grid=(count, GROUP // 2),
            in_specs=[wide, wide] + [block] * 6 + [pl.BlockSpec(memory_space=pl.ANY)] * len(before),
            out_specs=[wide, wide] + [block] * 5,
            scratch_shapes=[
                pltpu.VMEM((window, ROWS), F32),
                pltpu.VMEM((window, HEAD_WIDTH), BF16),
                pltpu.VMEM((window, HEAD_WIDTH), BF16),
                pltpu.VMEM((HEAD_WIDTH, window), BF16),
                pltpu.VMEM((HEAD_WIDTH, window), BF16),
                pltpu.VMEM((window, HEAD_WIDTH), F32),
                pltpu.VMEM((window, HEAD_WIDTH), F32),
            ],
        ),
        out_shape=[whole, whole] + [part] * 5,
        input_output_aliases={10 + i: i for i in range(len(before))},
        name="context_rows",
    )(place, span_lengths, q, g, *blocks, *before)


def question_scores(place_ref, ring, k, q):
    s = dot_nt(k, q) * SCALE2
    lane = lax.broadcasted_iota(jnp.int32, (1, 2 * ROWS), 1) % ROWS
    x, y = lane // 32, lane // 8 % 4
    piece = jnp.where(x % 2 == 0, x * 2 + y, 8 + y // 2 * 4 + y % 2 + (3 - x))
    row = CONTEXT + place_ref[0] // 32 * ROWS + piece * 8 + lane % 8
    key = ring_of(place_ref[0], ring) * RING + lax.broadcasted_iota(jnp.int32, s.shape, 0)
    return jnp.where(key <= row, s, HIDDEN)


def ring_of(place, ring):
    return (place // 32 + 4 - ring) % 4 * 4 + place // 8 % 4


def question_pair(qg_ref, which):
    return stacked(qg_ref[:, which].reshape(ROWS, 2 * HEAD_WIDTH))


def ring_keys(kv_ref):
    return kv_ref[0, :, 0].reshape(RING, HEAD_WIDTH), kv_ref[0, :, 1].reshape(RING, HEAD_WIDTH)


def statistics_kernel(place_ref, qg_ref, kv_ref, stats_ref):
    pair, ring = pl.program_id(0), pl.program_id(1)
    k, v = ring_keys(kv_ref)
    q = question_pair(qg_ref, 0)
    g = question_pair(qg_ref, 1)
    s = question_scores(place_ref, ring, k, q)
    slots = [pl.ds(pl.multiple_of(part * GROUP, GROUP) + pair, 1) for part in range(3)]

    @pl.when(ring == 0)
    def _():
        stats_ref[slots[0], :] = jnp.full((1, 2 * ROWS), FLOOR, F32)
        stats_ref[slots[1], :] = jnp.zeros((1, 2 * ROWS), F32)
        stats_ref[slots[2], :] = jnp.zeros((1, 2 * ROWS), F32)

    before = stats_ref[slots[0], :]
    top = jnp.maximum(before, jnp.max(s, axis=0, keepdims=True))
    factor = jnp.exp2(before - top)
    w = jnp.exp2(s - top)
    stats_ref[slots[0], :] = top
    stats_ref[slots[1], :] = stats_ref[slots[1], :] * factor + jnp.sum(w, axis=0, keepdims=True)
    dd = jnp.sum(w * dot_nt(v, g), axis=0, keepdims=True)
    stats_ref[slots[2], :] = stats_ref[slots[2], :] * factor + dd


def question_kernel(
    place_ref, qg_ref, kv_ref, stats_ref, part_ref, dkv_ref, k_t, v_t, dk_acc, dv_acc, out_acc, dq_acc
):
    ring, pair = pl.program_id(0), pl.program_id(1)
    k, v = ring_keys(kv_ref)

    @pl.when(pair == 0)
    def _():
        k_t[...] = k.T
        v_t[...] = v.T
        dk_acc[...] = jnp.zeros_like(dk_acc)
        dv_acc[...] = jnp.zeros_like(dv_acc)

    @pl.when(ring == 0)
    def _():
        out_acc[pair] = jnp.zeros((HEAD_WIDTH, 2 * ROWS), F32)
        dq_acc[pair] = jnp.zeros((HEAD_WIDTH, 2 * ROWS), F32)

    q = question_pair(qg_ref, 0)
    g = question_pair(qg_ref, 1)
    s = question_scores(place_ref, ring, k, q)
    lse = stats_ref[pl.ds(pair, 1), :]
    dd = stats_ref[pl.ds(GROUP + pair, 1), :]
    p = jnp.exp2(s - lse)
    ds = (p * (dot_nt(v, g) - dd)).astype(BF16)
    pb = p.astype(BF16)
    out_acc[pair] += dot_nn(v_t[...], pb)
    dq_acc[pair] += dot_nn(k_t[...], ds)
    dv_acc[...] += dot_nn(pb, g)
    dk_acc[...] += dot_nn(ds, q)

    @pl.when(ring == 3)
    def _():
        shape = (16, 8, 2 * HEAD_WIDTH)
        part_ref[:, 0] = unstacked(out_acc[pair]).reshape(shape)
        part_ref[:, 1] = unstacked(dq_acc[pair] * SCALE).reshape(shape)

    @pl.when(pair == GROUP // 2 - 1)
    def _():
        dkv_ref[0, :, 0] = (dk_acc[...] * SCALE).astype(BF16).reshape(8, ROWS, HEAD_WIDTH)
        dkv_ref[0, :, 1] = dv_acc[...].astype(BF16).reshape(8, ROWS, HEAD_WIDTH)


def question_statistics(place, qg, kv):
    return pl.pallas_call(
        statistics_kernel,
        grid_spec=pltpu.PrefetchScalarGridSpec(
            num_scalar_prefetch=1,
            grid=(GROUP // 2, 4),
            in_specs=[
                pl.BlockSpec((16, 2, 8, 2 * HEAD_WIDTH), lambda h, r, *_: (0, 0, 0, h)),
                pl.BlockSpec((1, 8, 2, ROWS, HEAD_WIDTH), lambda h, r, *_: (r, 0, 0, 0, 0)),
            ],
            out_specs=pl.BlockSpec((3 * GROUP, 2 * ROWS), lambda h, r, *_: (0, 0)),
        ),
        out_shape=jax.ShapeDtypeStruct((3 * GROUP, 2 * ROWS), F32),
        name="question_statistics",
    )(place, qg, kv)


def question_attention(place, qg, kv, stats):
    rows = pl.BlockSpec((16, 2, 8, 2 * HEAD_WIDTH), lambda r, h, *_: (0, 0, 0, h))
    keys = pl.BlockSpec((1, 8, 2, ROWS, HEAD_WIDTH), lambda r, h, *_: (r, 0, 0, 0, 0))
    last_rows = pl.BlockSpec(
        (16, 2, 8, 2 * HEAD_WIDTH), lambda r, h, *_: (0, 0, 0, jnp.where(r == 3, h, 0))
    )
    return pl.pallas_call(
        question_kernel,
        grid_spec=pltpu.PrefetchScalarGridSpec(
            num_scalar_prefetch=1,
            grid=(4, GROUP // 2),
            in_specs=[rows, keys, pl.BlockSpec((2 * GROUP, 2 * ROWS), lambda r, h, *_: (0, 0))],
            out_specs=[last_rows, keys],
            scratch_shapes=[
                pltpu.VMEM((HEAD_WIDTH, RING), BF16),
                pltpu.VMEM((HEAD_WIDTH, RING), BF16),
                pltpu.VMEM((RING, HEAD_WIDTH), F32),
                pltpu.VMEM((RING, HEAD_WIDTH), F32),
                pltpu.VMEM((GROUP // 2, HEAD_WIDTH, 2 * ROWS), F32),
                pltpu.VMEM((GROUP // 2, HEAD_WIDTH, 2 * ROWS), F32),
            ],
        ),
        out_shape=[
            jax.ShapeDtypeStruct(qg.shape, BF16),
            jax.ShapeDtypeStruct(kv.shape, BF16),
        ],
        name="question_rows",
    )(place, qg, kv, stats)


def copied(sources, targets, done):
    for pairs in (sources, targets):
        copies = [pltpu.make_async_copy(a, b, done.at[i]) for i, (a, b) in enumerate(pairs)]
        for copy in copies:
            copy.start()
        for copy in copies:
            copy.wait()


def move_call(kernel, place, arrays, shapes, room, copies, aliases=None):
    anywhere = pl.BlockSpec(memory_space=pl.ANY)
    return pl.pallas_call(
        kernel,
        grid_spec=pltpu.PrefetchScalarGridSpec(
            num_scalar_prefetch=1,
            grid=(1,),
            in_specs=[anywhere] * len(arrays),
            out_specs=[anywhere] * len(shapes),
            scratch_shapes=[pltpu.VMEM(room, BF16), pltpu.SemaphoreType.DMA((copies,))],
        ),
        out_shape=[jax.ShapeDtypeStruct(shape, BF16) for shape in shapes],
        input_output_aliases=aliases or {},
    )(place, *arrays)


def pieces_kernel(place_ref, q_ref, g_ref, p0, p1, p2, p3, room, done):
    @pl.when(place_ref[0] >= CONTEXT // ROWS)
    def _():
        targets = []
        for j, piece in enumerate((p0, p1, p2, p3)):
            for t in range(4):
                for which in range(2):
                    rows = pl.ds(32 * j + 8 * t, 8)
                    targets.append((room.at[which, rows], piece.at[t, which]))
        copied([(q_ref, room.at[0]), (g_ref, room.at[1])], targets, done)


def question_pieces(place, q, g):
    width = q.shape[1]
    return move_call(pieces_kernel, place, (q, g), [(4, 2, 8, width)] * 4, (2, ROWS, width), 32)


def spokes_kernel(place_ref, p0, p1, p2, p3, s0, s1, s2, s3, room, done):
    ring = place_ref[0] // 8
    for hub, piece, members in zip(HUBS, (p0, p1, p2, p3), QUADRANTS):

        @pl.when((ring == hub[0] * 4 + hub[1]) & (place_ref[0] % 8 >= 4))
        def _():
            first = members.index(hub)
            targets = [(room.at[(first + d) % 4], s) for d, s in enumerate((s0, s1, s2, s3))]
            copied([(piece, room)], targets, done)


def question_spokes(place, pieces):
    shape = pieces[0].shape
    return move_call(spokes_kernel, place, pieces, [shape[1:]] * 4, shape, 4)


def pick_kernel(place_ref, s0, s1, s2, s3, deal_ref, room, done):
    x, y = place_ref[0] // 32, place_ref[0] // 8 % 4
    step = jnp.where(x % 2 == 0, (y + 1) % 4, y % 2 + 3 - x)
    wide = GROUP * HEAD_WIDTH
    for d, piece in enumerate((s0, s1, s2, s3)):

        @pl.when((step == d) & (place_ref[0] % 8 >= 4))
        def _():
            groups = range(KEY_VALUE_HEADS)
            targets = [(room.at[:, :, pl.ds(k * wide, wide)], deal_ref.at[k]) for k in groups]
            copied([(piece, room)], targets, done)


def question_pick(place, spokes):
    shape = spokes[0].shape
    deal = (KEY_VALUE_HEADS, 2, 8, GROUP * HEAD_WIDTH)
    return move_call(pick_kernel, place, spokes, [deal], shape, KEY_VALUE_HEADS)[0]


def results_kernel(place_ref, out_in, dq_in, b0, b1, b2, b3, out_ref, dq_ref, room, done):
    @pl.when(place_ref[0] >= CONTEXT // ROWS)
    def _():
        sources, targets = [], []
        for j, back in enumerate((b0, b1, b2, b3)):
            sources.append((back, room.at[j]))
            for t in range(4):
                for which, ref in enumerate((out_ref, dq_ref)):
                    rows = pl.ds(32 * j + 8 * t, 8)
                    targets.append((room.at[j, t, which], ref.at[rows]))
        copied(sources, targets, done)


def question_results(place, out, dq, back):
    return move_call(
        results_kernel, place, (out, dq, *back), [out.shape] * 2,
        (4,) + back[0].shape, 32, {1: 0, 2: 1},
    )


def permuted(block, pairs):
    index = [place % 16 * 8 + place // 16 for place in range(DEVICES)]
    return lax.ppermute(block, MESH_AXES, [(index[i], index[j]) for i, j in pairs])


def shifted(block, distance):
    pairs = [(i, i + distance) for i in range(CONTEXT // ROWS)]
    return permuted(block, [(i, j) for i, j in pairs if 0 <= j < CONTEXT // ROWS])


def swapped(block):
    return permuted(block, [(i, i ^ 1) for i in range(DEVICES)])


def turned(block, distance):
    return permuted(block, [(i, (i + 32 * distance) % DEVICES) for i in range(DEVICES)])


def in_ring(ring, holder):
    return (ring[0] * 4 + ring[1]) * 8 + 4 + holder


def hub_pairs(j):
    return [(DEVICES - 4 + o, in_ring(HUBS[j], o)) for o in range(4)]


def spoke_pairs(d):
    pairs = []
    for hub, members in zip(HUBS, QUADRANTS):
        member = members[(members.index(hub) + d) % 4]
        pairs += [(in_ring(hub, o), in_ring(member, o)) for o in range(4)]
    return pairs


def back_to_front(pairs):
    return [(j, i) for i, j in pairs]


def exchanged(blocks, axes):
    return lax.all_to_all(blocks, axes, split_axis=0, concat_axis=0, tiled=True)


def merged(stats):
    parts = exchanged(jnp.broadcast_to(stats, (4,) + stats.shape), ("yh", "yl"))
    tops, totals, sums = jnp.split(parts, 3, axis=1)
    top = jnp.max(tops, axis=0)
    factor = jnp.exp2(tops - top)
    total = jnp.sum(totals * factor, axis=0)
    return jnp.concatenate([top + jnp.log2(total), jnp.sum(sums * factor, axis=0) / total])


def added(*terms):
    return sum(t.astype(F32) for t in terms)


def shards(q, k, v, g, span_lengths):
    place = lax.axis_index(AXES)
    place_arg = place.reshape(1).astype(jnp.int32)
    even = place % 2 == 0
    even_x = place // 32 % 2 == 0
    wide = GROUP * HEAD_WIDTH
    barrier = lax.optimization_barrier

    def headed(a):
        return a.reshape(ROWS, KEY_VALUE_HEADS, HEAD_WIDTH).transpose(1, 0, 2)

    kv = jnp.stack([headed(k), headed(v)], axis=1)
    kv_ring = exchanged(kv, ("z", "c"))
    pieces = question_pieces(place_arg, q, g)
    pieces = [permuted(pieces[j], hub_pairs(j)) for j in range(4)]
    same1 = shifted(kv, 2)
    same2 = shifted(same1, 2)
    blocks = (kv, same1, same2, swapped(kv), swapped(same1), swapped(same2))

    pieces, blocks = barrier((pieces, blocks))
    spokes = question_spokes(place_arg, pieces)
    spokes = [spokes[0]] + [permuted(spokes[d], spoke_pairs(d)) for d in (1, 2, 3)]
    context = context_attention(0, 2, place_arg, span_lengths, q, g, blocks)
    spokes, kv_ring, context = barrier((spokes, kv_ring, context))
    kv_ring = [kv_ring] + [turned(kv_ring, i) for i in (1, 2, 3)]
    deal = exchanged(question_pick(place_arg, spokes), ("z", "c"))
    context = context_attention(2, 2, place_arg, span_lengths, q, g, blocks, context)
    deal, context = barrier((deal, context))
    own = jnp.broadcast_to(deal[4:, None], (4, 4, 2, 8, wide))
    qg = exchanged(own.reshape(16, 2, 8, wide), PLANE)
    context = context_attention(4, 2, place_arg, span_lengths, q, g, blocks, context)
    qg, kv_ring, context = barrier((qg, jnp.stack(kv_ring), context))

    stats = question_statistics(place_arg, qg, kv_ring)
    stats, context = barrier((stats, context))
    context = context_attention(6, 2, place_arg, span_lengths, q, g, blocks, context)
    stats, context = barrier((merged(stats), context))
    parts, dkv_ring = question_attention(place_arg, qg, kv_ring, stats)
    parts, dkv_ring, context = barrier((parts, dkv_ring, context))
    out, dq, d0, d1, d2, d3, d4 = context
    from1, from3 = swapped(d1), swapped(d3)
    none = jnp.zeros_like(d1)
    far = shifted(added(d4, jnp.where(even, none, from3)).astype(BF16), -2)
    near = shifted(added(d2, jnp.where(even, from3, from1), far).astype(BF16), -2)

    parts = exchanged(parts, PLANE)
    parts = jnp.sum(parts.reshape(4, 4, 2, 8, wide).astype(F32), axis=1).astype(BF16)
    parts = exchanged(jnp.concatenate([jnp.zeros_like(parts), parts]), ("z", "c"))
    parts, dkv_ring = barrier((parts, dkv_ring))
    mine = parts.transpose(1, 2, 0, 3).reshape(2, 8, KEY_VALUE_HEADS * wide)
    gathered = [permuted(mine, back_to_front(spoke_pairs(d))) for d in (1, 2, 3)]
    hub = jnp.where(even_x, jnp.stack(gathered + [mine]), jnp.stack([mine] + gathered))
    back = [permuted(hub, back_to_front(hub_pairs(j))) for j in range(4)]

    turns = [turned(dkv_ring[i], -i) for i in (1, 2, 3)]
    dkv_ring = added(dkv_ring[0], *turns)
    dkv_ring = exchanged(dkv_ring.astype(BF16), ("z", "c"))
    dkv = added(d0, jnp.where(even, from1, none), near, dkv_ring).astype(BF16)
    dk = dkv[:, 0].transpose(1, 0, 2).reshape(k.shape)
    dv = dkv[:, 1].transpose(1, 0, 2).reshape(v.shape)

    out, dq = question_results(place_arg, out, dq, back)
    return out, dq, dk, dv


def solution(mesh):
    grid = Mesh(mesh.devices.reshape(2, 4, 2, 4, 2), MESH_AXES)
    rows = P(AXES, None)
    return jax.shard_map(
        shards,
        mesh=grid,
        in_specs=(rows, rows, rows, rows, P()),
        out_specs=(rows,) * 4,
        check_vma=False,
    )
```

```python
import math

import jax
import jax.numpy as jnp
from jax import lax
from jax.experimental import pallas as pl
from jax.experimental.pallas import tpu as pltpu
from jax.sharding import Mesh
from jax.sharding import PartitionSpec as P


QUERY_HEADS = 64
KEY_VALUE_HEADS = 8
HEAD_WIDTH = 128
GROUP = QUERY_HEADS // KEY_VALUE_HEADS
QLEN = 512
ROWS = 128
BACK = 4
SPANS = 62
AXES = ("x", "yh", "yl", "z", "c")
MESH_AXES = ("yl", "z", "c", "x", "yh")
PLANE = ("x", "yh", "yl")
DEVICES = 128
CONTEXT = DEVICES * ROWS - QLEN
RING = 8 * ROWS
SCALE = 1.0 / math.sqrt(HEAD_WIDTH)
SCALE2 = SCALE * math.log2(math.e)
HIDDEN = -1e30
FLOOR = -1e29
BF16 = jnp.bfloat16
F32 = jnp.float32


HUBS = ((0, 3), (2, 3), (3, 0), (3, 2))
QUADRANTS = (
    ((0, 0), (0, 1), (0, 2), (0, 3)),
    ((2, 0), (2, 1), (2, 2), (2, 3)),
    ((3, 0), (3, 1), (1, 0), (1, 1)),
    ((3, 2), (3, 3), (1, 2), (1, 3)),
)


def dot_nt(a, b):
    return lax.dot_general(a, b, (((1,), (1,)), ((), ())), preferred_element_type=F32)


def dot_nn(a, b):
    return lax.dot_general(a, b, (((1,), (0,)), ((), ())), preferred_element_type=F32)


def stacked(pair):
    return jnp.concatenate([pair[:, :HEAD_WIDTH], pair[:, HEAD_WIDTH:]], axis=0)


def unstacked(transposed):
    rows = transposed.T
    return jnp.concatenate([rows[:ROWS], rows[ROWS:]], axis=1).astype(BF16)


def context_kernel(
    place_ref, span_ref, q_ref, g_ref, same0, same1, same2, swapped0, swapped1, swapped2, *rest,
):
    rest = rest[-16:]
    out_ref, dq_ref, d0, d1, d2, d3, d4, bias, k_win, v_win, k_t, v_t, p_all, ds_all, q_all, g_all = rest
    window = (BACK + 1) * ROWS
    group, pair = pl.program_id(0), pl.program_id(1)
    place = place_ref[0]

    @pl.when((group == 0) & (pair == 0))
    def _():
        row = place * ROWS + lax.broadcasted_iota(jnp.int32, (1, ROWS), 1)

        def step(n, carry):
            begin, start = carry
            start = jnp.where(row >= begin, begin, start)
            return begin + span_ref[n], start

        _, start = lax.fori_loop(0, SPANS, step, (jnp.int32(0), jnp.zeros((1, ROWS), jnp.int32)))
        start = jnp.where(row >= CONTEXT, DEVICES * ROWS, start)
        key = (place - BACK) * ROWS + lax.broadcasted_iota(jnp.int32, (window, ROWS), 0)
        bias[...] = jnp.where((key >= start) & (key <= row), 0.0, HIDDEN)

    def fill(i, ref):
        k_win[i * ROWS : (i + 1) * ROWS] = ref[0, 0]
        v_win[i * ROWS : (i + 1) * ROWS] = ref[0, 1]
        k_t[:, i * ROWS : (i + 1) * ROWS] = ref[0, 0].T
        v_t[:, i * ROWS : (i + 1) * ROWS] = ref[0, 1].T

    @pl.when(pair == 0)
    def _():
        fill(0, same2)
        fill(2, same1)
        fill(4, same0)

    @pl.when((pair == 0) & (place % 2 == 0))
    def _():
        fill(1, swapped2)
        fill(3, swapped1)

    @pl.when((pair == 0) & (place % 2 == 1))
    def _():
        fill(1, swapped1)
        fill(3, swapped0)

    hide = jnp.concatenate([bias[...], bias[...]], axis=1)
    kw, vw = k_win[...], v_win[...]
    for n in range(GROUP // 2):
        cols = slice(2 * n * HEAD_WIDTH, 2 * (n + 1) * HEAD_WIDTH)
        lanes = slice(2 * n * ROWS, 2 * (n + 1) * ROWS)
        q = stacked(q_ref[:, cols])
        g = stacked(g_ref[:, cols])
        s = dot_nt(kw, q) * SCALE2 + hide
        dp = dot_nt(vw, g)
        top = jnp.maximum(jnp.max(s, axis=0, keepdims=True), FLOOR)
        w = jnp.exp2(s - top)
        total = jnp.sum(w, axis=0, keepdims=True)
        p = w * jnp.where(total > 0.0, 1.0 / total, 0.0)
        dd = jnp.sum(p * dp, axis=0, keepdims=True)
        ds = (p * (dp - dd)).astype(BF16)
        pb = p.astype(BF16)
        out_ref[:, cols] = unstacked(dot_nn(v_t[...], pb))
        dq_ref[:, cols] = unstacked(dot_nn(k_t[...], ds) * SCALE)
        p_all[:, lanes] = pb
        ds_all[:, lanes] = ds
        q_all[lanes] = q
        g_all[lanes] = g
    dk = dot_nn(ds_all[...], q_all[...]) * SCALE
    dv = dot_nn(p_all[...], g_all[...])
    for i, ref in enumerate((d4, d3, d2, d1, d0)):
        ref[0, 0] = dk[i * ROWS : (i + 1) * ROWS].astype(BF16)
        ref[0, 1] = dv[i * ROWS : (i + 1) * ROWS].astype(BF16)


def context_attention(first, count, place, span_lengths, q, g, blocks, before=()):
    window = (BACK + 1) * ROWS
    wide = pl.BlockSpec((ROWS, GROUP * HEAD_WIDTH), lambda a, b, *_: (0, a + first))
    block = pl.BlockSpec((1, 2, ROWS, HEAD_WIDTH), lambda a, b, *_: (a + first, 0, 0, 0))
    whole = jax.ShapeDtypeStruct(q.shape, BF16)
    part = jax.ShapeDtypeStruct((KEY_VALUE_HEADS, 2, ROWS, HEAD_WIDTH), BF16)
    return pl.pallas_call(
        context_kernel,
        grid_spec=pltpu.PrefetchScalarGridSpec(
            num_scalar_prefetch=2,
            grid=(count, 1),
            in_specs=[wide, wide] + [block] * 6 + [pl.BlockSpec(memory_space=pl.ANY)] * len(before),
            out_specs=[wide, wide] + [block] * 5,
            scratch_shapes=[
                pltpu.VMEM((window, ROWS), F32),
                pltpu.VMEM((window, HEAD_WIDTH), BF16),
                pltpu.VMEM((window, HEAD_WIDTH), BF16),
                pltpu.VMEM((HEAD_WIDTH, window), BF16),
                pltpu.VMEM((HEAD_WIDTH, window), BF16),
                pltpu.VMEM((window, GROUP * ROWS), BF16),
                pltpu.VMEM((window, GROUP * ROWS), BF16),
                pltpu.VMEM((GROUP * ROWS, HEAD_WIDTH), BF16),
                pltpu.VMEM((GROUP * ROWS, HEAD_WIDTH), BF16),
            ],
        ),
        out_shape=[whole, whole] + [part] * 5,
        input_output_aliases={10 + i: i for i in range(len(before))},
        name="context_rows",
    )(place, span_lengths, q, g, *blocks, *before)


def question_scores(place_ref, ring, k, q):
    s = dot_nt(k, q) * SCALE2
    lane = lax.broadcasted_iota(jnp.int32, (1, 2 * ROWS), 1) % ROWS
    x, y = lane // 32, lane // 8 % 4
    piece = jnp.where(x % 2 == 0, x * 2 + y, 8 + y // 2 * 4 + y % 2 + (3 - x))
    row = CONTEXT + place_ref[0] // 32 * ROWS + piece * 8 + lane % 8
    key = ring_of(place_ref[0], ring) * RING + lax.broadcasted_iota(jnp.int32, s.shape, 0)
    return jnp.where(key <= row, s, HIDDEN)


def ring_of(place, ring):
    return (place // 32 + 4 - ring) % 4 * 4 + place // 8 % 4


def question_pair(qg_ref, which):
    return stacked(qg_ref[:, which].reshape(ROWS, 2 * HEAD_WIDTH))


def ring_keys(kv_ref):
    return kv_ref[0, :, 0].reshape(RING, HEAD_WIDTH), kv_ref[0, :, 1].reshape(RING, HEAD_WIDTH)


def statistics_kernel(place_ref, qg_ref, kv_ref, stats_ref):
    pair, ring = pl.program_id(0), pl.program_id(1)
    k, v = ring_keys(kv_ref)
    q = question_pair(qg_ref, 0)
    g = question_pair(qg_ref, 1)
    s = question_scores(place_ref, ring, k, q)
    slots = [pl.ds(pl.multiple_of(part * GROUP, GROUP) + pair, 1) for part in range(3)]

    @pl.when(ring == 0)
    def _():
        stats_ref[slots[0], :] = jnp.full((1, 2 * ROWS), FLOOR, F32)
        stats_ref[slots[1], :] = jnp.zeros((1, 2 * ROWS), F32)
        stats_ref[slots[2], :] = jnp.zeros((1, 2 * ROWS), F32)

    before = stats_ref[slots[0], :]
    top = jnp.maximum(before, jnp.max(s, axis=0, keepdims=True))
    factor = jnp.exp2(before - top)
    w = jnp.exp2(s - top)
    stats_ref[slots[0], :] = top
    stats_ref[slots[1], :] = stats_ref[slots[1], :] * factor + jnp.sum(w, axis=0, keepdims=True)
    dd = jnp.sum(w * dot_nt(v, g), axis=0, keepdims=True)
    stats_ref[slots[2], :] = stats_ref[slots[2], :] * factor + dd


def question_kernel(
    place_ref, qg_ref, kv_ref, stats_ref, part_ref, dkv_ref, k_t, v_t, dk_acc, dv_acc, out_acc, dq_acc
):
    ring, pair = pl.program_id(0), pl.program_id(1)
    k, v = ring_keys(kv_ref)

    @pl.when(pair == 0)
    def _():
        k_t[...] = k.T
        v_t[...] = v.T
        dk_acc[...] = jnp.zeros_like(dk_acc)
        dv_acc[...] = jnp.zeros_like(dv_acc)

    @pl.when(ring == 0)
    def _():
        out_acc[pair] = jnp.zeros((HEAD_WIDTH, 2 * ROWS), F32)
        dq_acc[pair] = jnp.zeros((HEAD_WIDTH, 2 * ROWS), F32)

    q = question_pair(qg_ref, 0)
    g = question_pair(qg_ref, 1)
    s = question_scores(place_ref, ring, k, q)
    lse = stats_ref[pl.ds(pair, 1), :]
    dd = stats_ref[pl.ds(GROUP + pair, 1), :]
    p = jnp.exp2(s - lse)
    ds = (p * (dot_nt(v, g) - dd)).astype(BF16)
    pb = p.astype(BF16)
    out_acc[pair] += dot_nn(v_t[...], pb)
    dq_acc[pair] += dot_nn(k_t[...], ds)
    dv_acc[...] += dot_nn(pb, g)
    dk_acc[...] += dot_nn(ds, q)

    @pl.when(ring == 3)
    def _():
        shape = (16, 8, 2 * HEAD_WIDTH)
        part_ref[:, 0] = unstacked(out_acc[pair]).reshape(shape)
        part_ref[:, 1] = unstacked(dq_acc[pair] * SCALE).reshape(shape)

    @pl.when(pair == GROUP // 2 - 1)
    def _():
        dkv_ref[0, :, 0] = (dk_acc[...] * SCALE).astype(BF16).reshape(8, ROWS, HEAD_WIDTH)
        dkv_ref[0, :, 1] = dv_acc[...].astype(BF16).reshape(8, ROWS, HEAD_WIDTH)


def question_statistics(place, qg, kv):
    return pl.pallas_call(
        statistics_kernel,
        grid_spec=pltpu.PrefetchScalarGridSpec(
            num_scalar_prefetch=1,
            grid=(GROUP // 2, 4),
            in_specs=[
                pl.BlockSpec((16, 2, 8, 2 * HEAD_WIDTH), lambda h, r, *_: (0, 0, 0, h)),
                pl.BlockSpec((1, 8, 2, ROWS, HEAD_WIDTH), lambda h, r, *_: (r, 0, 0, 0, 0)),
            ],
            out_specs=pl.BlockSpec((3 * GROUP, 2 * ROWS), lambda h, r, *_: (0, 0)),
        ),
        out_shape=jax.ShapeDtypeStruct((3 * GROUP, 2 * ROWS), F32),
        name="question_statistics",
    )(place, qg, kv)


def question_attention(place, qg, kv, stats):
    rows = pl.BlockSpec((16, 2, 8, 2 * HEAD_WIDTH), lambda r, h, *_: (0, 0, 0, h))
    keys = pl.BlockSpec((1, 8, 2, ROWS, HEAD_WIDTH), lambda r, h, *_: (r, 0, 0, 0, 0))
    last_rows = pl.BlockSpec(
        (16, 2, 8, 2 * HEAD_WIDTH), lambda r, h, *_: (0, 0, 0, jnp.where(r == 3, h, 0))
    )
    return pl.pallas_call(
        question_kernel,
        grid_spec=pltpu.PrefetchScalarGridSpec(
            num_scalar_prefetch=1,
            grid=(4, GROUP // 2),
            in_specs=[rows, keys, pl.BlockSpec((2 * GROUP, 2 * ROWS), lambda r, h, *_: (0, 0))],
            out_specs=[last_rows, keys],
            scratch_shapes=[
                pltpu.VMEM((HEAD_WIDTH, RING), BF16),
                pltpu.VMEM((HEAD_WIDTH, RING), BF16),
                pltpu.VMEM((RING, HEAD_WIDTH), F32),
                pltpu.VMEM((RING, HEAD_WIDTH), F32),
                pltpu.VMEM((GROUP // 2, HEAD_WIDTH, 2 * ROWS), F32),
                pltpu.VMEM((GROUP // 2, HEAD_WIDTH, 2 * ROWS), F32),
            ],
        ),
        out_shape=[
            jax.ShapeDtypeStruct(qg.shape, BF16),
            jax.ShapeDtypeStruct(kv.shape, BF16),
        ],
        name="question_rows",
    )(place, qg, kv, stats)


def copied(sources, targets, done):
    for pairs in (sources, targets):
        copies = [pltpu.make_async_copy(a, b, done.at[i]) for i, (a, b) in enumerate(pairs)]
        for copy in copies:
            copy.start()
        for copy in copies:
            copy.wait()


def move_call(kernel, place, arrays, shapes, room, copies, aliases=None):
    anywhere = pl.BlockSpec(memory_space=pl.ANY)
    return pl.pallas_call(
        kernel,
        grid_spec=pltpu.PrefetchScalarGridSpec(
            num_scalar_prefetch=1,
            grid=(1,),
            in_specs=[anywhere] * len(arrays),
            out_specs=[anywhere] * len(shapes),
            scratch_shapes=[pltpu.VMEM(room, BF16), pltpu.SemaphoreType.DMA((copies,))],
        ),
        out_shape=[jax.ShapeDtypeStruct(shape, BF16) for shape in shapes],
        input_output_aliases=aliases or {},
    )(place, *arrays)


def pieces_kernel(place_ref, q_ref, g_ref, p0, p1, p2, p3, room, done):
    @pl.when(place_ref[0] >= CONTEXT // ROWS)
    def _():
        targets = []
        for j, piece in enumerate((p0, p1, p2, p3)):
            for t in range(4):
                for which in range(2):
                    rows = pl.ds(32 * j + 8 * t, 8)
                    targets.append((room.at[which, rows], piece.at[t, which]))
        copied([(q_ref, room.at[0]), (g_ref, room.at[1])], targets, done)


def question_pieces(place, q, g):
    width = q.shape[1]
    return move_call(pieces_kernel, place, (q, g), [(4, 2, 8, width)] * 4, (2, ROWS, width), 32)


def spokes_kernel(place_ref, p0, p1, p2, p3, s0, s1, s2, s3, room, done):
    ring = place_ref[0] // 8
    for hub, piece, members in zip(HUBS, (p0, p1, p2, p3), QUADRANTS):

        @pl.when((ring == hub[0] * 4 + hub[1]) & (place_ref[0] % 8 >= 4))
        def _():
            first = members.index(hub)
            targets = [(room.at[(first + d) % 4], s) for d, s in enumerate((s0, s1, s2, s3))]
            copied([(piece, room)], targets, done)


def question_spokes(place, pieces):
    shape = pieces[0].shape
    return move_call(spokes_kernel, place, pieces, [shape[1:]] * 4, shape, 4)


def pick_kernel(place_ref, s0, s1, s2, s3, deal_ref, room, done):
    x, y = place_ref[0] // 32, place_ref[0] // 8 % 4
    step = jnp.where(x % 2 == 0, (y + 1) % 4, y % 2 + 3 - x)
    wide = GROUP * HEAD_WIDTH
    for d, piece in enumerate((s0, s1, s2, s3)):

        @pl.when((step == d) & (place_ref[0] % 8 >= 4))
        def _():
            groups = range(KEY_VALUE_HEADS)
            targets = [(room.at[:, :, pl.ds(k * wide, wide)], deal_ref.at[k]) for k in groups]
            copied([(piece, room)], targets, done)


def question_pick(place, spokes):
    shape = spokes[0].shape
    deal = (KEY_VALUE_HEADS, 2, 8, GROUP * HEAD_WIDTH)
    return move_call(pick_kernel, place, spokes, [deal], shape, KEY_VALUE_HEADS)[0]


def results_kernel(place_ref, out_in, dq_in, b0, b1, b2, b3, out_ref, dq_ref, room, done):
    @pl.when(place_ref[0] >= CONTEXT // ROWS)
    def _():
        sources, targets = [], []
        for j, back in enumerate((b0, b1, b2, b3)):
            sources.append((back, room.at[j]))
            for t in range(4):
                for which, ref in enumerate((out_ref, dq_ref)):
                    rows = pl.ds(32 * j + 8 * t, 8)
                    targets.append((room.at[j, t, which], ref.at[rows]))
        copied(sources, targets, done)


def question_results(place, out, dq, back):
    return move_call(
        results_kernel, place, (out, dq, *back), [out.shape] * 2,
        (4,) + back[0].shape, 32, {1: 0, 2: 1},
    )


def permuted(block, pairs):
    index = [place % 16 * 8 + place // 16 for place in range(DEVICES)]
    return lax.ppermute(block, MESH_AXES, [(index[i], index[j]) for i, j in pairs])


def shifted(block, distance):
    pairs = [(i, i + distance) for i in range(CONTEXT // ROWS)]
    return permuted(block, [(i, j) for i, j in pairs if 0 <= j < CONTEXT // ROWS])


def swapped(block):
    return permuted(block, [(i, i ^ 1) for i in range(DEVICES)])


def turned(block, distance):
    return permuted(block, [(i, (i + 32 * distance) % DEVICES) for i in range(DEVICES)])


def in_ring(ring, holder):
    return (ring[0] * 4 + ring[1]) * 8 + 4 + holder


def hub_pairs(j):
    return [(DEVICES - 4 + o, in_ring(HUBS[j], o)) for o in range(4)]


def spoke_pairs(d):
    pairs = []
    for hub, members in zip(HUBS, QUADRANTS):
        member = members[(members.index(hub) + d) % 4]
        pairs += [(in_ring(hub, o), in_ring(member, o)) for o in range(4)]
    return pairs


def back_to_front(pairs):
    return [(j, i) for i, j in pairs]


def exchanged(blocks, axes):
    return lax.all_to_all(blocks, axes, split_axis=0, concat_axis=0, tiled=True)


def merged(stats):
    parts = exchanged(jnp.broadcast_to(stats, (4,) + stats.shape), ("yh", "yl"))
    tops, totals, sums = jnp.split(parts, 3, axis=1)
    top = jnp.max(tops, axis=0)
    factor = jnp.exp2(tops - top)
    total = jnp.sum(totals * factor, axis=0)
    return jnp.concatenate([top + jnp.log2(total), jnp.sum(sums * factor, axis=0) / total])


def added(*terms):
    return sum(t.astype(F32) for t in terms)


def shards(q, k, v, g, span_lengths):
    place = lax.axis_index(AXES)
    place_arg = place.reshape(1).astype(jnp.int32)
    even = place % 2 == 0
    even_x = place // 32 % 2 == 0
    wide = GROUP * HEAD_WIDTH
    barrier = lax.optimization_barrier

    def headed(a):
        return a.reshape(ROWS, KEY_VALUE_HEADS, HEAD_WIDTH).transpose(1, 0, 2)

    kv = jnp.stack([headed(k), headed(v)], axis=1)
    kv_ring = exchanged(kv, ("z", "c"))
    pieces = question_pieces(place_arg, q, g)
    dealt = {}
    for j in range(4):
        dealt[j] = permuted(pieces[j], hub_pairs(j))
    pieces = [dealt[j] for j in range(4)]
    same1 = shifted(kv, 2)
    same2 = shifted(same1, 2)
    blocks = (kv, same1, same2, swapped(kv), swapped(same1), swapped(same2))

    pieces, blocks = barrier((pieces, blocks))
    spokes = question_spokes(place_arg, pieces)
    spokes = [spokes[0]] + [permuted(spokes[d], spoke_pairs(d)) for d in (1, 2, 3)]
    context = context_attention(0, 2, place_arg, span_lengths, q, g, blocks)
    spokes, kv_ring, context = barrier((spokes, kv_ring, context))
    kv_ring = [kv_ring] + [turned(kv_ring, i) for i in (1, 2, 3)]
    deal = exchanged(question_pick(place_arg, spokes), ("z", "c"))
    context = context_attention(2, 2, place_arg, span_lengths, q, g, blocks, context)
    deal, context = barrier((deal, context))
    own = jnp.broadcast_to(deal[4:, None], (4, 4, 2, 8, wide))
    qg = exchanged(own.reshape(16, 2, 8, wide), PLANE)
    context = context_attention(4, 2, place_arg, span_lengths, q, g, blocks, context)
    qg, kv_ring, context = barrier((qg, jnp.stack(kv_ring), context))

    stats = question_statistics(place_arg, qg, kv_ring)
    stats, context = barrier((stats, context))
    context = context_attention(6, 2, place_arg, span_lengths, q, g, blocks, context)
    stats, context = barrier((merged(stats), context))
    parts, dkv_ring = question_attention(place_arg, qg, kv_ring, stats)
    parts, dkv_ring, context = barrier((parts, dkv_ring, context))
    out, dq, d0, d1, d2, d3, d4 = context
    from1, from3 = swapped(d1), swapped(d3)
    none = jnp.zeros_like(d1)
    far = shifted(added(d4, jnp.where(even, none, from3)).astype(BF16), -2)
    near = shifted(added(d2, jnp.where(even, from3, from1), far).astype(BF16), -2)

    parts = exchanged(parts, PLANE)
    parts = jnp.sum(parts.reshape(4, 4, 2, 8, wide).astype(F32), axis=1).astype(BF16)
    parts = exchanged(jnp.concatenate([jnp.zeros_like(parts), parts]), ("z", "c"))
    parts, dkv_ring = barrier((parts, dkv_ring))
    mine = parts.transpose(1, 2, 0, 3).reshape(2, 8, KEY_VALUE_HEADS * wide)
    gathered = [permuted(mine, back_to_front(spoke_pairs(d))) for d in (1, 2, 3)]
    hub = jnp.where(even_x, jnp.stack(gathered + [mine]), jnp.stack([mine] + gathered))
    back = [permuted(hub, back_to_front(hub_pairs(j))) for j in range(4)]

    turns = [turned(dkv_ring[i], -i) for i in (1, 2, 3)]
    dkv_ring = added(dkv_ring[0], *turns)
    dkv_ring = exchanged(dkv_ring.astype(BF16), ("z", "c"))
    dkv = added(d0, jnp.where(even, from1, none), near, dkv_ring).astype(BF16)
    dk = dkv[:, 0].transpose(1, 0, 2).reshape(k.shape)
    dv = dkv[:, 1].transpose(1, 0, 2).reshape(v.shape)

    out, dq = question_results(place_arg, out, dq, back)
    return out, dq, dk, dv


def solution(mesh):
    grid = Mesh(mesh.devices.reshape(2, 4, 2, 4, 2), MESH_AXES)
    rows = P(AXES, None)
    return jax.shard_map(
        shards,
        mesh=grid,
        in_specs=(rows, rows, rows, rows, P()),
        out_specs=(rows,) * 4,
        check_vma=False,
    )
```

```python
import math

import jax
import jax.numpy as jnp
from jax import lax
from jax.experimental import pallas as pl
from jax.experimental.pallas import tpu as pltpu
from jax.sharding import Mesh
from jax.sharding import PartitionSpec as P


QUERY_HEADS = 64
KEY_VALUE_HEADS = 8
HEAD_WIDTH = 128
GROUP = QUERY_HEADS // KEY_VALUE_HEADS
QLEN = 512
ROWS = 128
BACK = 4
SPANS = 62
AXES = ("x", "yh", "yl", "z", "c")
MESH_AXES = ("yl", "z", "c", "x", "yh")
PLANE = ("x", "yh", "yl")
DEVICES = 128
CONTEXT = DEVICES * ROWS - QLEN
RING = 8 * ROWS
SCALE = 1.0 / math.sqrt(HEAD_WIDTH)
SCALE2 = SCALE * math.log2(math.e)
HIDDEN = -1e30
FLOOR = -1e29
PAIRS = 2
BF16 = jnp.bfloat16
F32 = jnp.float32


HUBS = ((0, 3), (2, 3), (3, 0), (3, 2))
QUADRANTS = (
    ((0, 0), (0, 1), (0, 2), (0, 3)),
    ((2, 0), (2, 1), (2, 2), (2, 3)),
    ((3, 0), (3, 1), (1, 0), (1, 1)),
    ((3, 2), (3, 3), (1, 2), (1, 3)),
)


def dot_nt(a, b):
    return lax.dot_general(a, b, (((1,), (1,)), ((), ())), preferred_element_type=F32)


def dot_nn(a, b):
    return lax.dot_general(a, b, (((1,), (0,)), ((), ())), preferred_element_type=F32)


def stacked(pair):
    return jnp.concatenate([pair[:, :HEAD_WIDTH], pair[:, HEAD_WIDTH:]], axis=0)


def unstacked(transposed):
    rows = transposed.T
    return jnp.concatenate([rows[:ROWS], rows[ROWS:]], axis=1).astype(BF16)


def context_kernel(
    place_ref, span_ref, q_ref, g_ref, same0, same1, same2, swapped0, swapped1, swapped2, *rest,
):
    rest = rest[-16:]
    out_ref, dq_ref, d0, d1, d2, d3, d4, bias, k_win, v_win, k_t, v_t, p_all, ds_all, q_all, g_all = rest
    window = (BACK + 1) * ROWS
    group, pair = pl.program_id(0), pl.program_id(1)
    place = place_ref[0]

    @pl.when((group == 0) & (pair == 0))
    def _():
        row = place * ROWS + lax.broadcasted_iota(jnp.int32, (1, ROWS), 1)

        def step(n, carry):
            begin, start = carry
            start = jnp.where(row >= begin, begin, start)
            return begin + span_ref[n], start

        _, start = lax.fori_loop(0, SPANS, step, (jnp.int32(0), jnp.zeros((1, ROWS), jnp.int32)))
        start = jnp.where(row >= CONTEXT, DEVICES * ROWS, start)
        key = (place - BACK) * ROWS + lax.broadcasted_iota(jnp.int32, (window, ROWS), 0)
        bias[...] = jnp.where((key >= start) & (key <= row), 0.0, HIDDEN)

    def fill(i, ref):
        k_win[i * ROWS : (i + 1) * ROWS] = ref[0, 0]
        v_win[i * ROWS : (i + 1) * ROWS] = ref[0, 1]
        k_t[:, i * ROWS : (i + 1) * ROWS] = ref[0, 0].T
        v_t[:, i * ROWS : (i + 1) * ROWS] = ref[0, 1].T

    @pl.when(pair == 0)
    def _():
        fill(0, same2)
        fill(2, same1)
        fill(4, same0)

    @pl.when((pair == 0) & (place % 2 == 0))
    def _():
        fill(1, swapped2)
        fill(3, swapped1)

    @pl.when((pair == 0) & (place % 2 == 1))
    def _():
        fill(1, swapped1)
        fill(3, swapped0)

    hide = jnp.concatenate([bias[...], bias[...]], axis=1)
    kw, vw = k_win[...], v_win[...]
    for n in range(GROUP // 2):
        cols = slice(2 * n * HEAD_WIDTH, 2 * (n + 1) * HEAD_WIDTH)
        lanes = slice(2 * n * ROWS, 2 * (n + 1) * ROWS)
        q = stacked(q_ref[:, cols])
        g = stacked(g_ref[:, cols])
        s = dot_nt(kw, q) * SCALE2 + hide
        dp = dot_nt(vw, g)
        top = jnp.maximum(jnp.max(s, axis=0, keepdims=True), FLOOR)
        w = jnp.exp2(s - top)
        total = jnp.sum(w, axis=0, keepdims=True)
        p = w * jnp.where(total > 0.0, 1.0 / total, 0.0)
        dd = jnp.sum(p * dp, axis=0, keepdims=True)
        ds = (p * (dp - dd)).astype(BF16)
        pb = p.astype(BF16)
        out_ref[:, cols] = unstacked(dot_nn(v_t[...], pb))
        dq_ref[:, cols] = unstacked(dot_nn(k_t[...], ds) * SCALE)
        p_all[:, lanes] = pb
        ds_all[:, lanes] = ds
        q_all[lanes] = q
        g_all[lanes] = g
    dk = dot_nn(ds_all[...], q_all[...]) * SCALE
    dv = dot_nn(p_all[...], g_all[...])
    for i, ref in enumerate((d4, d3, d2, d1, d0)):
        ref[0, 0] = dk[i * ROWS : (i + 1) * ROWS].astype(BF16)
        ref[0, 1] = dv[i * ROWS : (i + 1) * ROWS].astype(BF16)


def context_attention(first, count, place, span_lengths, q, g, blocks, before=()):
    window = (BACK + 1) * ROWS
    wide = pl.BlockSpec((ROWS, GROUP * HEAD_WIDTH), lambda a, b, *_: (0, a + first))
    block = pl.BlockSpec((1, 2, ROWS, HEAD_WIDTH), lambda a, b, *_: (a + first, 0, 0, 0))
    whole = jax.ShapeDtypeStruct(q.shape, BF16)
    part = jax.ShapeDtypeStruct((KEY_VALUE_HEADS, 2, ROWS, HEAD_WIDTH), BF16)
    return pl.pallas_call(
        context_kernel,
        grid_spec=pltpu.PrefetchScalarGridSpec(
            num_scalar_prefetch=2,
            grid=(count, 1),
            in_specs=[wide, wide] + [block] * 6 + [pl.BlockSpec(memory_space=pl.ANY)] * len(before),
            out_specs=[wide, wide] + [block] * 5,
            scratch_shapes=[
                pltpu.VMEM((window, ROWS), F32),
                pltpu.VMEM((window, HEAD_WIDTH), BF16),
                pltpu.VMEM((window, HEAD_WIDTH), BF16),
                pltpu.VMEM((HEAD_WIDTH, window), BF16),
                pltpu.VMEM((HEAD_WIDTH, window), BF16),
                pltpu.VMEM((window, GROUP * ROWS), BF16),
                pltpu.VMEM((window, GROUP * ROWS), BF16),
                pltpu.VMEM((GROUP * ROWS, HEAD_WIDTH), BF16),
                pltpu.VMEM((GROUP * ROWS, HEAD_WIDTH), BF16),
            ],
        ),
        out_shape=[whole, whole] + [part] * 5,
        input_output_aliases={10 + i: i for i in range(len(before))},
        name="context_rows",
    )(place, span_lengths, q, g, *blocks, *before)


def question_scores(place_ref, ring, k, q):
    s = dot_nt(k, q) * SCALE2
    lane = lax.broadcasted_iota(jnp.int32, (1, 2 * ROWS), 1) % ROWS
    x, y = lane // 32, lane // 8 % 4
    piece = jnp.where(x % 2 == 0, x * 2 + y, 8 + y // 2 * 4 + y % 2 + (3 - x))
    row = CONTEXT + place_ref[0] // 32 * ROWS + piece * 8 + lane % 8
    key = ring_of(place_ref[0], ring) * RING + lax.broadcasted_iota(jnp.int32, s.shape, 0)
    return jnp.where(key <= row, s, HIDDEN)


def ring_of(place, ring):
    return (place // 32 + 4 - ring) % 4 * 4 + place // 8 % 4


def question_pair(qg_ref, which, n):
    part = qg_ref[:, which, :, 2 * n * HEAD_WIDTH : 2 * (n + 1) * HEAD_WIDTH]
    return stacked(part.reshape(ROWS, 2 * HEAD_WIDTH))


def ring_keys(kv_ref):
    return kv_ref[0, :, 0].reshape(RING, HEAD_WIDTH), kv_ref[0, :, 1].reshape(RING, HEAD_WIDTH)


def statistics_kernel(place_ref, qg_ref, kv_ref, stats_ref):
    half, ring = pl.program_id(0), pl.program_id(1)
    k, v = ring_keys(kv_ref)

    @pl.when((ring == 0) & (half == 0))
    def _():
        stats_ref[:GROUP] = jnp.full((GROUP, 2 * ROWS), FLOOR, F32)
        stats_ref[GROUP:] = jnp.zeros((2 * GROUP, 2 * ROWS), F32)

    for n in range(PAIRS):
        q = question_pair(qg_ref, 0, n)
        g = question_pair(qg_ref, 1, n)
        s = question_scores(place_ref, ring, k, q)
        dp = dot_nt(v, g)
        slots = [pl.ds(part * GROUP + PAIRS * half + n, 1) for part in range(3)]
        before = stats_ref[slots[0], :]
        top = jnp.maximum(before, jnp.max(s, axis=0, keepdims=True))
        factor = jnp.exp2(before - top)
        w = jnp.exp2(s - top)
        total = jnp.sum(w, axis=0, keepdims=True)
        dd = jnp.sum(w * dp, axis=0, keepdims=True)
        stats_ref[slots[0], :] = top
        stats_ref[slots[1], :] = stats_ref[slots[1], :] * factor + total
        stats_ref[slots[2], :] = stats_ref[slots[2], :] * factor + dd


def question_kernel(
    place_ref, qg_ref, kv_ref, stats_ref, part_ref, dkv_ref, k_t, v_t, dk_acc, dv_acc, out_acc, dq_acc
):
    ring, half = pl.program_id(0), pl.program_id(1)
    k, v = ring_keys(kv_ref)

    @pl.when(half == 0)
    def _():
        k_t[...] = k.T
        v_t[...] = v.T
        dk_acc[...] = jnp.zeros_like(dk_acc)
        dv_acc[...] = jnp.zeros_like(dv_acc)

    @pl.when((ring == 0) & (half == 0))
    def _():
        out_acc[...] = jnp.zeros_like(out_acc)
        dq_acc[...] = jnp.zeros_like(dq_acc)

    all_q, all_g, all_p, all_ds = [], [], [], []
    for n in range(PAIRS):
        pair = PAIRS * half + n
        q = question_pair(qg_ref, 0, n)
        g = question_pair(qg_ref, 1, n)
        s = question_scores(place_ref, ring, k, q)
        dp = dot_nt(v, g)
        lse = stats_ref[pl.ds(pair, 1), :]
        dd = stats_ref[pl.ds(GROUP + pair, 1), :]
        p = jnp.exp2(s - lse)
        ds = (p * (dp - dd)).astype(BF16)
        pb = p.astype(BF16)
        out_acc[pair] += dot_nn(v_t[...], pb)
        dq_acc[pair] += dot_nn(k_t[...], ds)
        all_q.append(q)
        all_g.append(g)
        all_p.append(pb)
        all_ds.append(ds)
    dv_acc[...] += dot_nn(jnp.concatenate(all_p, axis=1), jnp.concatenate(all_g, axis=0))
    dk_acc[...] += dot_nn(jnp.concatenate(all_ds, axis=1), jnp.concatenate(all_q, axis=0))

    @pl.when(ring == 3)
    def _():
        shape = (16, 8, 2 * HEAD_WIDTH)
        for n in range(PAIRS):
            pair = PAIRS * half + n
            cols = slice(2 * n * HEAD_WIDTH, 2 * (n + 1) * HEAD_WIDTH)
            part_ref[:, 0, :, cols] = unstacked(out_acc[pair]).reshape(shape)
            part_ref[:, 1, :, cols] = unstacked(dq_acc[pair] * SCALE).reshape(shape)

    @pl.when(half == GROUP // 2 // PAIRS - 1)
    def _():
        dkv_ref[0, :, 0] = (dk_acc[...] * SCALE).astype(BF16).reshape(8, ROWS, HEAD_WIDTH)
        dkv_ref[0, :, 1] = dv_acc[...].astype(BF16).reshape(8, ROWS, HEAD_WIDTH)


def question_statistics(place, qg, kv):
    return pl.pallas_call(
        statistics_kernel,
        grid_spec=pltpu.PrefetchScalarGridSpec(
            num_scalar_prefetch=1,
            grid=(GROUP // 2 // PAIRS, 4),
            in_specs=[
                pl.BlockSpec((16, 2, 8, 2 * PAIRS * HEAD_WIDTH), lambda h, r, *_: (0, 0, 0, h)),
                pl.BlockSpec((1, 8, 2, ROWS, HEAD_WIDTH), lambda h, r, *_: (r, 0, 0, 0, 0)),
            ],
            out_specs=pl.BlockSpec((3 * GROUP, 2 * ROWS), lambda h, r, *_: (0, 0)),
        ),
        out_shape=jax.ShapeDtypeStruct((3 * GROUP, 2 * ROWS), F32),
        name="question_statistics",
    )(place, qg, kv)


def question_attention(place, qg, kv, stats):
    rows = pl.BlockSpec((16, 2, 8, 2 * PAIRS * HEAD_WIDTH), lambda r, h, *_: (0, 0, 0, h))
    keys = pl.BlockSpec((1, 8, 2, ROWS, HEAD_WIDTH), lambda r, h, *_: (r, 0, 0, 0, 0))
    last_rows = pl.BlockSpec(
        (16, 2, 8, 2 * PAIRS * HEAD_WIDTH), lambda r, h, *_: (0, 0, 0, jnp.where(r == 3, h, 0))
    )
    return pl.pallas_call(
        question_kernel,
        grid_spec=pltpu.PrefetchScalarGridSpec(
            num_scalar_prefetch=1,
            grid=(4, GROUP // 2 // PAIRS),
            in_specs=[rows, keys, pl.BlockSpec((2 * GROUP, 2 * ROWS), lambda r, h, *_: (0, 0))],
            out_specs=[last_rows, keys],
            scratch_shapes=[
                pltpu.VMEM((HEAD_WIDTH, RING), BF16),
                pltpu.VMEM((HEAD_WIDTH, RING), BF16),
                pltpu.VMEM((RING, HEAD_WIDTH), F32),
                pltpu.VMEM((RING, HEAD_WIDTH), F32),
                pltpu.VMEM((GROUP // 2, HEAD_WIDTH, 2 * ROWS), F32),
                pltpu.VMEM((GROUP // 2, HEAD_WIDTH, 2 * ROWS), F32),
            ],
        ),
        out_shape=[
            jax.ShapeDtypeStruct(qg.shape, BF16),
            jax.ShapeDtypeStruct(kv.shape, BF16),
        ],
        name="question_rows",
    )(place, qg, kv, stats)


def copied(sources, targets, done):
    for pairs in (sources, targets):
        copies = [pltpu.make_async_copy(a, b, done.at[i]) for i, (a, b) in enumerate(pairs)]
        for copy in copies:
            copy.start()
        for copy in copies:
            copy.wait()


def move_call(kernel, place, arrays, shapes, room, copies, aliases=None):
    anywhere = pl.BlockSpec(memory_space=pl.ANY)
    return pl.pallas_call(
        kernel,
        grid_spec=pltpu.PrefetchScalarGridSpec(
            num_scalar_prefetch=1,
            grid=(1,),
            in_specs=[anywhere] * len(arrays),
            out_specs=[anywhere] * len(shapes),
            scratch_shapes=[pltpu.VMEM(room, BF16), pltpu.SemaphoreType.DMA((copies,))],
        ),
        out_shape=[jax.ShapeDtypeStruct(shape, BF16) for shape in shapes],
        input_output_aliases=aliases or {},
    )(place, *arrays)


def pieces_kernel(place_ref, q_ref, g_ref, p0, p1, p2, p3, room, done):
    @pl.when(place_ref[0] >= CONTEXT // ROWS)
    def _():
        targets = []
        for j, piece in enumerate((p0, p1, p2, p3)):
            for t in range(4):
                for which in range(2):
                    rows = pl.ds(32 * j + 8 * t, 8)
                    targets.append((room.at[which, rows], piece.at[t, which]))
        copied([(q_ref, room.at[0]), (g_ref, room.at[1])], targets, done)


def question_pieces(place, q, g):
    width = q.shape[1]
    return move_call(pieces_kernel, place, (q, g), [(4, 2, 8, width)] * 4, (2, ROWS, width), 32)


def spokes_kernel(place_ref, p0, p1, p2, p3, s0, s1, s2, s3, room, done):
    ring = place_ref[0] // 8
    for hub, piece, members in zip(HUBS, (p0, p1, p2, p3), QUADRANTS):

        @pl.when((ring == hub[0] * 4 + hub[1]) & (place_ref[0] % 8 >= 4))
        def _():
            first = members.index(hub)
            targets = [(room.at[(first + d) % 4], s) for d, s in enumerate((s0, s1, s2, s3))]
            copied([(piece, room)], targets, done)


def question_spokes(place, pieces):
    shape = pieces[0].shape
    return move_call(spokes_kernel, place, pieces, [shape[1:]] * 4, shape, 4)


def pick_kernel(place_ref, s0, s1, s2, s3, deal_ref, room, done):
    x, y = place_ref[0] // 32, place_ref[0] // 8 % 4
    step = jnp.where(x % 2 == 0, (y + 1) % 4, y % 2 + 3 - x)
    wide = GROUP * HEAD_WIDTH
    for d, piece in enumerate((s0, s1, s2, s3)):

        @pl.when((step == d) & (place_ref[0] % 8 >= 4))
        def _():
            groups = range(KEY_VALUE_HEADS)
            targets = [(room.at[:, :, pl.ds(k * wide, wide)], deal_ref.at[k]) for k in groups]
            copied([(piece, room)], targets, done)


def question_pick(place, spokes):
    shape = spokes[0].shape
    deal = (KEY_VALUE_HEADS, 2, 8, GROUP * HEAD_WIDTH)
    return move_call(pick_kernel, place, spokes, [deal], shape, KEY_VALUE_HEADS)[0]


def results_kernel(place_ref, out_in, dq_in, b0, b1, b2, b3, out_ref, dq_ref, room, done):
    @pl.when(place_ref[0] >= CONTEXT // ROWS)
    def _():
        sources, targets = [], []
        for j, back in enumerate((b0, b1, b2, b3)):
            sources.append((back, room.at[j]))
            for t in range(4):
                for which, ref in enumerate((out_ref, dq_ref)):
                    rows = pl.ds(32 * j + 8 * t, 8)
                    targets.append((room.at[j, t, which], ref.at[rows]))
        copied(sources, targets, done)


def question_results(place, out, dq, back):
    return move_call(
        results_kernel, place, (out, dq, *back), [out.shape] * 2,
        (4,) + back[0].shape, 32, {1: 0, 2: 1},
    )


def permuted(block, pairs):
    index = [place % 16 * 8 + place // 16 for place in range(DEVICES)]
    return lax.ppermute(block, MESH_AXES, [(index[i], index[j]) for i, j in pairs])


def shifted(block, distance):
    pairs = [(i, i + distance) for i in range(CONTEXT // ROWS)]
    return permuted(block, [(i, j) for i, j in pairs if 0 <= j < CONTEXT // ROWS])


def swapped(block):
    return permuted(block, [(i, i ^ 1) for i in range(DEVICES)])


def turned(block, distance):
    return permuted(block, [(i, (i + 32 * distance) % DEVICES) for i in range(DEVICES)])


def in_ring(ring, holder):
    return (ring[0] * 4 + ring[1]) * 8 + 4 + holder


def hub_pairs(j):
    return [(DEVICES - 4 + o, in_ring(HUBS[j], o)) for o in range(4)]


def spoke_pairs(d):
    pairs = []
    for hub, members in zip(HUBS, QUADRANTS):
        member = members[(members.index(hub) + d) % 4]
        pairs += [(in_ring(hub, o), in_ring(member, o)) for o in range(4)]
    return pairs


def back_to_front(pairs):
    return [(j, i) for i, j in pairs]


def exchanged(blocks, axes):
    return lax.all_to_all(blocks, axes, split_axis=0, concat_axis=0, tiled=True)


def merged(stats):
    parts = exchanged(jnp.broadcast_to(stats, (4,) + stats.shape), ("yh", "yl"))
    tops, totals, sums = jnp.split(parts, 3, axis=1)
    top = jnp.max(tops, axis=0)
    factor = jnp.exp2(tops - top)
    total = jnp.sum(totals * factor, axis=0)
    return jnp.concatenate([top + jnp.log2(total), jnp.sum(sums * factor, axis=0) / total])


def added(*terms):
    return sum(t.astype(F32) for t in terms)


def shards(q, k, v, g, span_lengths):
    place = lax.axis_index(AXES)
    place_arg = place.reshape(1).astype(jnp.int32)
    even = place % 2 == 0
    even_x = place // 32 % 2 == 0
    wide = GROUP * HEAD_WIDTH
    barrier = lax.optimization_barrier

    def headed(a):
        return a.reshape(ROWS, KEY_VALUE_HEADS, HEAD_WIDTH).transpose(1, 0, 2)

    kv = jnp.stack([headed(k), headed(v)], axis=1)
    kv_ring = exchanged(kv, ("z", "c"))
    pieces = question_pieces(place_arg, q, g)
    dealt = {}
    for j in range(4):
        dealt[j] = permuted(pieces[j], hub_pairs(j))
    pieces = [dealt[j] for j in range(4)]
    same1 = shifted(kv, 2)
    same2 = shifted(same1, 2)
    swapped1 = swapped(same1)
    blocks = (kv, same1, same2, swapped(kv), swapped1, swapped(same2))

    context = context_attention(0, 2, place_arg, span_lengths, q, g, blocks)
    pieces, kv_ring, context = barrier((pieces, kv_ring, context))
    kv_ring = [kv_ring] + [turned(kv_ring, i) for i in (1, 2, 3)]
    spokes = question_spokes(place_arg, pieces)
    spokes = [spokes[0]] + [permuted(spokes[d], spoke_pairs(d)) for d in (1, 2, 3)]
    context = context_attention(2, 2, place_arg, span_lengths, q, g, blocks, context)
    spokes, context = barrier((spokes, context))
    deal = exchanged(question_pick(place_arg, spokes), ("z", "c"))
    deal, context = barrier((deal, context))
    own = jnp.broadcast_to(deal[4:, None], (4, 4, 2, 8, wide))
    qg = exchanged(own.reshape(16, 2, 8, wide), PLANE)
    context = context_attention(4, 2, place_arg, span_lengths, q, g, blocks, context)
    qg, kv_ring, context = barrier((qg, jnp.stack(kv_ring), context))

    stats = question_statistics(place_arg, qg, kv_ring)
    stats, context = barrier((stats, context))
    context = context_attention(6, 2, place_arg, span_lengths, q, g, blocks, context)
    stats, context = barrier((merged(stats), context))
    parts, dkv_ring = question_attention(place_arg, qg, kv_ring, stats)
    parts, dkv_ring, context = barrier((parts, dkv_ring, context))
    out, dq, d0, d1, d2, d3, d4 = context
    from1, from3 = swapped(d1), swapped(d3)
    none = jnp.zeros_like(d1)
    far = shifted(added(d4, jnp.where(even, none, from3)).astype(BF16), -2)
    near = shifted(added(d2, jnp.where(even, from3, from1), far).astype(BF16), -2)

    parts = exchanged(parts, PLANE)
    parts = jnp.sum(parts.reshape(4, 4, 2, 8, wide).astype(F32), axis=1).astype(BF16)
    parts = exchanged(jnp.concatenate([jnp.zeros_like(parts), parts]), ("z", "c"))
    mine = parts.transpose(1, 2, 0, 3).reshape(2, 8, KEY_VALUE_HEADS * wide)
    gathered = [permuted(mine, back_to_front(spoke_pairs(d))) for d in (1, 2, 3)]
    hub = jnp.where(even_x, jnp.stack(gathered + [mine]), jnp.stack([mine] + gathered))
    back = [permuted(hub, back_to_front(hub_pairs(j))) for j in range(4)]

    turns = [turned(dkv_ring[i], -i) for i in (1, 2, 3)]
    dkv_ring = added(dkv_ring[0], *turns)
    dkv_ring = exchanged(dkv_ring.astype(BF16), ("z", "c"))
    dkv = added(d0, jnp.where(even, from1, none), near, dkv_ring).astype(BF16)
    dk = dkv[:, 0].transpose(1, 0, 2).reshape(k.shape)
    dv = dkv[:, 1].transpose(1, 0, 2).reshape(v.shape)

    out, dq = question_results(place_arg, out, dq, back)
    return out, dq, dk, dv


def solution(mesh):
    grid = Mesh(mesh.devices.reshape(2, 4, 2, 4, 2), MESH_AXES)
    rows = P(AXES, None)
    return jax.shard_map(
        shards,
        mesh=grid,
        in_specs=(rows, rows, rows, rows, P()),
        out_specs=(rows,) * 4,
        check_vma=False,
    )
```
